128 devices in a mesh: dom: 16 (over y, x), sub: 8 (over z, core).
Axes of the slice: x: 4, y: 4, z: 4, core: 2. Of those that a mesh axis runs over, the one named last changes fastest.
Arguments:
- history: bfloat16 [4096, 64, 128], P(('dom', 'sub')), may hold values from -6 to 6
- send_list: int32 [128, 128, 1], P(('dom', 'sub')), may hold values from 0 to 31
- send_count: int32 [128, 128], P(('dom', 'sub')), may hold values from 0 to 1, as said below
- mixed_mass: bfloat16 [16384, 128, 128], P(('dom', 'sub')), may hold values from -0.5 to 0.5
- relay_list: int32 [128, 128, 1], P(('dom', 'sub')), may hold values from 0 to 127, as said below
- relay_target: int32 [128, 128, 1], P(('dom', 'sub')), may hold values from 0 to 63
- mass_diag: float32 [8192, 128, 128], P(('dom', 'sub')), as said below
- mass_next: float32 [8192, 128, 128], P(('dom', 'sub')), may hold values from -0.18 to 0.18
- coupling: int32 [8192], P(('dom', 'sub')), may hold values 0 or 1
- precond: float32 [8192, 128, 128], P(('dom', 'sub')), as said below
Outputs:
- solution: float32 [8192, 64, 128], P(('dom', 'sub'))
- residual: float32 [8192, 64, 128], P(('dom', 'sub'))
The draws below stay inside these ranges and needn't reach their ends.
Inputs may be any that keep to these rules, and one draw needn't show every extreme that they name: `send_count`: live slots are the first ones. Every sender fills all 1 slots for some peer, and in every draw some receiver gets 1 live slots from every sender. For each owner e, the entries of relay_list[e] are a permutation of 0 .. 127. `mass_diag`: each block is symmetric; the assembled mass matrix is symmetric positive definite. `precond`: each block is symmetric positive definite.
All inputs are finite; a program needn't handle non-finite values. No bound on the sum of `coupling` on one device may be relied on, other than what follows from the above.
Results may differ from the reference program's by a relative error of at most 0.0003.
Values may be sent and summed in bfloat16 or wider, within the bound.
A program may use at most 128 MiB of HBM per device.

```python
import math
import jax
import jax.numpy as jnp
from jax import lax

VALS = 64
BROWS = 128
OB = 32
CAP = 1
NB = 64
ITERS = 3
SB = 128
OLD_BLOCKS = 4096
SLOTS = 16384
NEW_BLOCKS = 8192
DEVICES = 128


def draw_send_count(key, part):
    first_key, second_key, third_key = jax.random.split(key, 3)
    counts = jax.random.randint(first_key, (DEVICES, DEVICES), 0, CAP + 1)
    favoured = jax.random.randint(second_key, (DEVICES, 1), 0, DEVICES)
    column = jax.random.randint(third_key, (), 0, DEVICES)
    peers = jnp.arange(DEVICES)
    counts = jnp.where(peers[None, :] == favoured, CAP, counts)
    counts = jnp.where(peers[None, :] == column, CAP, counts)
    return counts.astype(jnp.int32)


def shuffled(one_key):
    return jax.random.permutation(one_key, DEVICES * CAP)


def draw_relay_list(key, part):
    keys = jax.random.split(key, DEVICES)
    orders = jax.vmap(shuffled)(keys)
    return orders.reshape(DEVICES, DEVICES, CAP).astype(jnp.int32)


def diagonal_rates(key):
    rate_key = jax.random.fold_in(key, 7)
    rates = jnp.exp(jax.random.uniform(rate_key, (NEW_BLOCKS, BROWS), jnp.float32, math.log(3.0), math.log(24.0)))
    return rates


def symmetric_noise(key, salt, scale):
    noise = jax.random.normal(jax.random.fold_in(key, salt), (NEW_BLOCKS, BROWS, BROWS), jnp.float32) * scale
    return (noise + jnp.swapaxes(noise, 1, 2)) * math.sqrt(0.5)


def draw_mass_diag(key, part):
    rates = diagonal_rates(key)
    identity = jnp.eye(BROWS, dtype=jnp.float32)[None]
    return symmetric_noise(key, 11, 0.03) + rates[:, :, None] * identity


def draw_precond(key, part):
    rates = diagonal_rates(key)
    identity = jnp.eye(BROWS, dtype=jnp.float32)[None]
    return symmetric_noise(key, 13, 0.0008) + (1.0 / rates)[:, :, None] * identity


def plant(values, rng, smallest, top_value):
    shape = values.shape
    spot = [jax.random.randint(jax.random.fold_in(rng, axis), (), 0, shape[axis]) for axis in range(len(shape))]
    values = values.at[tuple(spot)].set(smallest)
    longest = shape.index(max(shape))
    spot[longest] = (spot[longest] + 1) % shape[longest]
    return values.at[tuple(spot)].set(top_value)


def shard_levels(own_key, dims, pieces, least, high):
    factor_of = 1.0
    for position, blocks in pieces:
        draws = jax.random.uniform(jax.random.fold_in(jax.random.fold_in(own_key, 6), position), (blocks,), jnp.float32, least / len(pieces), high / len(pieces))
        factor_of = factor_of * jnp.repeat(jnp.exp(draws), dims[position] // blocks).reshape((-1,) + (1,) * (len(dims) - 1 - position))
    return factor_of


def bell_draw(key, shape, spread, limit, pieces=(), held_as=jnp.bfloat16):
    array = jax.random.normal(key, shape, jnp.float32) * spread
    if len(pieces) > 0:
        array = shard_levels(key, shape, pieces, -0.22, 0.18) * array
    return jnp.clip(array, min=-limit, max=limit).astype(held_as)


def setup_inputs(seed: int = 0) -> dict:
    streams_of = jax.random.split(jax.random.key(seed), 11)
    return {
        "history": bell_draw(streams_of[0], (OLD_BLOCKS, VALS, BROWS), 1.0, 6.0, ((0, 128),)),
        "send_list": plant(jax.random.randint(streams_of[1], (DEVICES, DEVICES, CAP), 0, OB), jax.random.fold_in(streams_of[1], 1), 0, OB - 1).astype(jnp.int32),
        "send_count": draw_send_count(jax.random.fold_in(streams_of[10], 71), 0),
        "mixed_mass": bell_draw(streams_of[3], (SLOTS, BROWS, BROWS), BROWS ** -0.5, 0.5, ((0, 128),)),
        "relay_list": draw_relay_list(jax.random.fold_in(streams_of[10], 71), 0),
        "relay_target": plant(jax.random.randint(streams_of[5], (DEVICES, DEVICES, CAP), 0, NB), jax.random.fold_in(streams_of[5], 1), 0, NB - 1).astype(jnp.int32),
        "mass_diag": draw_mass_diag(jax.random.fold_in(streams_of[10], 71), 0),
        "mass_next": bell_draw(streams_of[7], (NEW_BLOCKS, BROWS, BROWS), 0.03, 0.18, ((0, 128),), jnp.float32),
        "coupling": plant((jax.random.randint(streams_of[8], (NEW_BLOCKS,), 0, 4) < 3).astype(jnp.int32), jax.random.fold_in(streams_of[8], 1), 0, 1),
        "precond": draw_precond(jax.random.fold_in(streams_of[10], 71), 0),
    }


def apply_mass(field, mass_diag, mass_next, links):
    highest = lax.Precision.HIGHEST
    carried = links * jnp.einsum('gvs,gsr->gvr', field, mass_next, precision=highest)
    zero_block = jnp.zeros_like(field[:1])
    ahead = jnp.concatenate([field[1:], zero_block], axis=0)
    behind = jnp.concatenate([zero_block, carried[:-1]], axis=0)
    own = jnp.einsum('gvs,grs->gvr', field, mass_diag, precision=highest)
    onward = links * jnp.einsum('gvs,grs->gvr', ahead, mass_next, precision=highest)
    return own + onward + behind


def precondition(field, precond):
    return jnp.einsum('gvs,grs->gvr', field, precond, precision=lax.Precision.HIGHEST)


def reference(history, send_list, send_count, mixed_mass, relay_list, relay_target, mass_diag, mass_next, coupling, precond):
    highest = lax.Precision.HIGHEST
    slot_index = jnp.arange(CAP, dtype=jnp.int32)
    device_index = jnp.arange(DEVICES, dtype=jnp.int32)
    mixing = mixed_mass.reshape(DEVICES, SB, BROWS, BROWS)

    def per_owner(rhs, owner):
        picks = send_list[:, owner, :]
        live = slot_index[None, :] < send_count[:, owner][:, None]
        source = (device_index[:, None] * OB + picks).astype(jnp.int32)
        blocks = jnp.where(live[:, :, None, None], history[source], jnp.zeros((), history.dtype))
        blocks = blocks.reshape(SB, VALS, BROWS).astype(jnp.float32)
        tiles = jnp.einsum('kvs,ksr->kvr', blocks, mixing[owner].astype(jnp.float32), precision=highest)
        sending = tiles[relay_list[owner].reshape(-1).astype(jnp.int32)]
        target = (device_index[:, None] * NB + relay_target[:, owner, :]).astype(jnp.int32)
        rhs = rhs.at[target.reshape(-1)].add(sending)
        return rhs, None

    start = jnp.zeros((NEW_BLOCKS, VALS, BROWS), jnp.float32)
    rhs = lax.scan(per_owner, start, device_index)[0]

    links = coupling.astype(jnp.float32)[:, None, None]
    solution = jnp.zeros_like(rhs)
    residual = rhs
    reduced = precondition(residual, precond)
    direction = reduced
    norm_now = jnp.sum(residual * reduced, axis=(0, 2))
    for iteration in range(ITERS):
        image = apply_mass(direction, mass_diag, mass_next, links)
        alpha = norm_now / jnp.sum(direction * image, axis=(0, 2))
        solution = solution + alpha[None, :, None] * direction
        residual = residual - alpha[None, :, None] * image
        reduced = precondition(residual, precond)
        norm_next = jnp.sum(residual * reduced, axis=(0, 2))
        direction = reduced + (norm_next / norm_now)[None, :, None] * direction
        norm_now = norm_next
    return solution, residual
```

```python
import jax
import jax.numpy as jnp
from jax import lax
from jax.experimental import pallas as pl
from jax.experimental.pallas import tpu as pltpu
from jax.sharding import PartitionSpec as P

MESH = pl.DeviceIdType.MESH
F32 = jnp.float32
BF16 = jnp.bfloat16
STEPS = 3
CHUNK = 4


def split(value):
    high = value.astype(BF16)
    low = (value - high.astype(F32)).astype(BF16)
    return high, low


def stacked(value):
    return jnp.concatenate(split(value), axis=0)


def product(left, weights, half):
    full = jnp.dot(left, weights, preferred_element_type=F32)
    top = full[:half] + full[half:]
    width = top.shape[1] // 2
    return top[:, :width] + top[:, width:]


def solve_kernel(
    shape,
    order_ref,
    same_ref,
    last_ref,
    have_ref,
    links_ref,
    tiles_hbm,
    diag_hbm,
    next_hbm,
    prec_hbm,
    x_hbm,
    res_hbm,
    tiles,
    stage,
    wa,
    wp,
    diag_a,
    diag_p,
    res,
    red,
    xs,
    halo,
    acc,
    trace,
    inv,
    red_src,
    red_dom,
    red_sub,
    tile_sem,
    stage_sem,
    halo_send,
    halo_recv,
    link_send,
    link_recv,
    dom_send,
    dom_recv,
    sub_send,
    sub_recv,
    out_sem,
):
    doms, subs, count, values, rows, slots = shape
    devices = doms * subs
    me_dom, me_sub = lax.axis_index("dom"), lax.axis_index("sub")
    me = me_dom * subs + me_sub
    after = lax.rem(me + 1, devices)
    before = lax.rem(me + devices - 1, devices)
    after_id = (after // subs, lax.rem(after, subs))
    before_id = (before // subs, lax.rem(before, subs))

    load_tiles = pltpu.make_async_copy(tiles_hbm, tiles, tile_sem)
    load_tiles.start()

    barrier = pltpu.get_barrier_semaphore()
    pl.semaphore_signal(barrier, inc=1, device_id=after_id, device_id_type=MESH)
    pl.semaphore_signal(barrier, inc=1, device_id=before_id, device_id_type=MESH)

    @pl.loop(1, doms)
    def _(j):
        pl.semaphore_signal(
            barrier, inc=1, device_id=(lax.rem(me_dom + j, doms), me_sub), device_id_type=MESH
        )

    @pl.loop(1, subs)
    def _(j):
        pl.semaphore_signal(
            barrier, inc=1, device_id=(me_dom, lax.rem(me_sub + j, subs)), device_id_type=MESH
        )

    sources = (diag_hbm, next_hbm, prec_hbm)

    def stage_copy(chunk, which):
        slot = lax.rem(chunk, 2)
        return pltpu.make_async_copy(
            sources[which].at[pl.ds(chunk * CHUNK, CHUNK)],
            stage.at[slot, which],
            stage_sem.at[slot, which],
        )

    for which in range(3):
        stage_copy(0, which).start()
    trace[...] = jnp.zeros_like(trace)
    row = lax.broadcasted_iota(jnp.int32, (rows, rows), 0)
    col = lax.broadcasted_iota(jnp.int32, (rows, rows), 1)
    eye = row == col
    chunks = count // CHUNK

    @pl.loop(0, chunks)
    def _(chunk):
        @pl.when(chunk + 1 < chunks)
        def _():
            for which in range(3):
                stage_copy(chunk + 1, which).start()

        for which in range(3):
            stage_copy(chunk, which).wait()
        slot = lax.rem(chunk, 2)

        @pl.loop(0, CHUNK)
        def _(i):
            g = chunk * CHUNK + i
            here = stage[slot, 0, i]
            onto = stage[slot, 1, i]
            prec = stage[slot, 2, i]
            trace[...] += jnp.sum((here * prec).reshape(rows // 8, 8, rows), axis=0)
            diag_a[g] = jnp.sum(jnp.where(eye, here, 0.0), axis=0, keepdims=True)
            diag_p[g] = jnp.sum(jnp.where(eye, prec, 0.0), axis=0, keepdims=True)
            high, low = split(jnp.where(eye, 0.0, here))
            wa[g, 0:rows, 0:rows] = high
            wa[g, 0:rows, rows : 2 * rows] = low
            wrap = jnp.logical_and(g == count - 1, me == devices - 1)
            link = jnp.where(wrap, 0.0, links_ref[g].astype(F32))
            onto = onto * link
            high, low = split(onto)
            wa[g + 1, 2 * rows : 3 * rows, 0:rows] = high
            wa[g + 1, 2 * rows : 3 * rows, rows : 2 * rows] = low
            high, low = split(onto.T)
            wa[g, rows : 2 * rows, 0:rows] = high
            wa[g, rows : 2 * rows, rows : 2 * rows] = low
            high, low = split(jnp.where(eye, 0.0, prec))
            wp[g, :, 0:rows] = high
            wp[g, :, rows : 2 * rows] = low

    pl.semaphore_wait(barrier, 2 + doms - 1 + subs - 1)

    def reduce_over(phase, value):
        def dom_copy(peer, slot):
            return pltpu.make_async_remote_copy(
                src_ref=red_src.at[phase, 0],
                dst_ref=red_dom.at[phase, slot],
                send_sem=dom_send.at[phase, peer],
                recv_sem=dom_recv.at[phase, slot],
                device_id=(peer, me_sub),
                device_id_type=MESH,
            )

        def sub_copy(peer, slot):
            return pltpu.make_async_remote_copy(
                src_ref=red_src.at[phase, 1],
                dst_ref=red_sub.at[phase, slot],
                send_sem=sub_send.at[phase, peer],
                recv_sem=sub_recv.at[phase, slot],
                device_id=(me_dom, peer),
                device_id_type=MESH,
            )

        red_src[phase, 0] = value
        red_dom[phase, me_dom] = value

        @pl.loop(1, doms)
        def _(j):
            dom_copy(lax.rem(me_dom + j, doms), me_dom).start()

        @pl.loop(1, doms)
        def _(j):
            other = lax.rem(me_dom + j, doms)
            dom_copy(other, other).wait_recv()

        total = red_dom[phase, 0]
        for j in range(1, doms):
            total = total + red_dom[phase, j]
        red_src[phase, 1] = total
        red_sub[phase, me_sub] = total

        @pl.loop(1, subs)
        def _(j):
            sub_copy(lax.rem(me_sub + j, subs), me_sub).start()

        @pl.loop(1, subs)
        def _(j):
            other = lax.rem(me_sub + j, subs)
            sub_copy(other, other).wait_recv()

        total = red_sub[phase, 0]
        for j in range(1, subs):
            total = total + red_sub[phase, j]

        @pl.loop(1, doms)
        def _(j):
            dom_copy(lax.rem(me_dom + j, doms), me_dom).wait_send()

        @pl.loop(1, subs)
        def _(j):
            sub_copy(lax.rem(me_sub + j, subs), me_sub).wait_send()

        return total

    link_copy = pltpu.make_async_remote_copy(
        src_ref=wa.at[count, pl.ds(2 * rows, rows)],
        dst_ref=wa.at[0, pl.ds(2 * rows, rows)],
        send_sem=link_send,
        recv_sem=link_recv,
        device_id=after_id,
        device_id_type=MESH,
    )
    link_copy.start()
    theta = reduce_over(0, trace[...])
    theta = jnp.sum(jnp.sum(theta, axis=0, keepdims=True), axis=1, keepdims=True)
    inv[...] = jnp.broadcast_to((1.0 * devices * count * rows) / theta, inv.shape)

    load_tiles.wait()
    acc[0] = jnp.zeros_like(acc[0])

    def add_tile(j, running):
        running = running * same_ref[j] + tiles[order_ref[j]]
        red[j] = running
        return running

    lax.fori_loop(0, slots, add_tile, jnp.zeros((values, rows), F32))

    @pl.loop(0, count)
    def _(g):
        res[0, g] = red[last_ref[g]] * have_ref[g]

    def precondition(g, k, value):
        out = product(stacked(value), wp[g], values) + value * diag_p[g]
        red[k * count + g] = out
        xs[k % 2, g + 1] = stacked(out)

    def apply_block(g, k, left, right):
        here = xs[k % 2, g + 1]
        image = product(jnp.concatenate([here, right, left], axis=1), wa[g], values)
        field = red[k * count + g]
        image = image + field * diag_a[g]
        now = res[k, g]
        later = now - image * inv[0:1]
        res[k + 1, g] = later
        step = now - later
        if k == 0:
            acc[0] += field * step
        if k == 1:
            acc[1] += field * (res[0, g] - now)
            acc[2] += field * step
        if k == 2:
            acc[3] += field * (res[1, g] - now)
            acc[4] += field * step
            acc[5] += red[g] * later
            acc[6] += red[count + g] * later
            acc[7] += field * later
        if k + 1 < STEPS:
            precondition(g, k + 1, later)

    def inner(g, k):
        apply_block(g, k, xs[k % 2, g], xs[k % 2, g + 2])

    def halo_copy(k, side):
        return pltpu.make_async_remote_copy(
            src_ref=xs.at[k % 2, count if side == 0 else 1],
            dst_ref=halo.at[k, side],
            send_sem=halo_send.at[k, side],
            recv_sem=halo_recv.at[k, side],
            device_id=after_id if side == 0 else before_id,
            device_id_type=MESH,
        )

    middle = count // 2
    acc[...] = jnp.zeros_like(acc)
    precondition(0, 0, res[0, 0])
    precondition(count - 1, 0, res[0, count - 1])

    @pl.loop(1, 9)
    def _(g):
        precondition(g, 0, res[0, g])

    halo_copy(0, 0).start()
    halo_copy(0, 1).start()

    @pl.loop(9, count - 1)
    def _(g):
        precondition(g, 0, res[0, g])

    link_copy.wait()
    for k in range(STEPS):

        @pl.loop(1, middle)
        def _(g):
            inner(g, k)

        halo_copy(k, 0).wait()
        halo_copy(k, 1).wait()
        apply_block(0, k, halo[k, 0], xs[k % 2, 2])
        apply_block(count - 1, k, xs[k % 2, count - 1], halo[k, 1])

        @pl.loop(middle, middle + 4)
        def _(g):
            inner(g, k)

        if k + 1 < STEPS:
            halo_copy(k + 1, 0).start()
            halo_copy(k + 1, 1).start()

        @pl.loop(middle + 4, count - 1)
        def _(g):
            inner(g, k)

    lane = lax.broadcasted_iota(jnp.int32, (values, rows), 1)
    packed = jnp.zeros((values, rows), F32)
    for j in range(8):
        packed = packed + jnp.where(lane == j, jnp.sum(acc[j], axis=1, keepdims=True), 0.0)
    packed = jnp.concatenate([packed, jnp.zeros((rows - values, rows), F32)], axis=0)
    total = reduce_over(1, packed.T[0:8])

    def over(top, bottom):
        usable = bottom != 0.0
        return jnp.where(usable, top / jnp.where(usable, bottom, 1.0), 0.0)

    g00, g10, g11, g21, g22 = (total[j : j + 1] for j in range(5))
    h0, h1, h2 = (-total[j : j + 1] for j in range(5, 8))
    l1, l2 = over(g10, g00), over(g11, g00)
    d1 = g11 - l1 * g10
    mix = g21 - l2 * g10
    l3 = over(mix, d1)
    d2 = g22 - l2 * g11 - l3 * mix
    y1 = h1 - l1 * h0
    y2 = h2 - l2 * h0 - l3 * y1
    e2 = over(y2, d2)
    e1 = over(y1, d1) - l3 * e2
    e0 = over(h0, g00) - l1 * e1 - l2 * e2
    weights = jnp.concatenate([e0, e1, e2, jnp.zeros((rows - 3, rows), F32)], axis=0).T
    e0 = jnp.broadcast_to(weights[0:values, 0:1], (values, rows))
    e1 = jnp.broadcast_to(weights[0:values, 1:2], (values, rows))
    e2 = jnp.broadcast_to(weights[0:values, 2:3], (values, rows))
    scale = inv[0:1]
    x0, x1, x2 = (1.0 - e0) * scale, (1.0 - e1) * scale, (1.0 - e2) * scale
    r1, r2, r3 = e1 - e0, e2 - e1, 1.0 - e2

    @pl.loop(0, count)
    def _(g):
        u0, u1, u2 = red[g], red[count + g], red[2 * count + g]
        red[g] = x0 * u0 + x1 * u1 + x2 * u2
        res[0, g] = e0 * res[0, g] + r1 * res[1, g] + r2 * res[2, g] + r3 * res[3, g]

    put_x = pltpu.make_async_copy(red.at[pl.ds(0, count)], x_hbm, out_sem.at[0])
    put_r = pltpu.make_async_copy(res.at[0], res_hbm, out_sem.at[1])
    put_x.start()
    put_r.start()
    put_x.wait()
    put_r.wait()


def mass_solve(order, same, last, have, links, tiles, mass_diag, mass_next, precond):
    doms, subs = lax.axis_size("dom"), lax.axis_size("sub")
    slots, values, rows = tiles.shape
    count = mass_diag.shape[0]
    shape = (doms, subs, count, values, rows, slots)

    def kernel(*refs):
        solve_kernel(shape, *refs)

    smem = pl.BlockSpec(memory_space=pltpu.SMEM)
    hbm = pl.BlockSpec(memory_space=pl.ANY)
    field = jax.ShapeDtypeStruct((count, values, rows), F32)
    dma = pltpu.SemaphoreType.DMA
    return pl.pallas_call(
        kernel,
        out_shape=(field, field),
        in_specs=[smem] * 5 + [hbm] * 4,
        out_specs=(hbm, hbm),
        scratch_shapes=[
            pltpu.VMEM((slots, values, rows), F32),
            pltpu.VMEM((2, 3, CHUNK, rows, rows), F32),
            pltpu.VMEM((count + 1, 3 * rows, 2 * rows), BF16),
            pltpu.VMEM((count, rows, 2 * rows), BF16),
            pltpu.VMEM((count, 1, rows), F32),
            pltpu.VMEM((count, 1, rows), F32),
            pltpu.VMEM((STEPS + 1, count, values, rows), F32),
            pltpu.VMEM((STEPS * count, values, rows), F32),
            pltpu.VMEM((2, count + 2, 2 * values, rows), BF16),
            pltpu.VMEM((STEPS, 2, 2 * values, rows), BF16),
            pltpu.VMEM((8, values, rows), F32),
            pltpu.VMEM((8, rows), F32),
            pltpu.VMEM((8, rows), F32),
            pltpu.VMEM((2, 2, 8, rows), F32),
            pltpu.VMEM((2, doms, 8, rows), F32),
            pltpu.VMEM((2, subs, 8, rows), F32),
            dma,
            dma((2, 3)),
            dma((STEPS, 2)),
            dma((STEPS, 2)),
            dma,
            dma,
            dma((2, doms)),
            dma((2, doms)),
            dma((2, subs)),
            dma((2, subs)),
            dma((2,)),
        ],
        compiler_params=pltpu.CompilerParams(
            collective_id=0, has_side_effects=True, vmem_limit_bytes=60 * 1024 * 1024
        ),
    )(order, same, last, have, links, tiles, mass_diag, mass_next, precond)


def target_order(targets, count):
    slots = targets.shape[0]
    spot = jnp.arange(slots, dtype=jnp.int32)
    key = targets * slots + spot
    rank = jnp.sum((key[None, :] < key[:, None]).astype(jnp.int32), axis=1)
    at = rank[None, :] == spot[:, None]
    order = jnp.sum(jnp.where(at, spot[None, :], 0), axis=1)
    ordered = jnp.sum(jnp.where(at, targets[None, :], 0), axis=1)
    same = jnp.concatenate([jnp.zeros((1,), F32), (ordered[1:] == ordered[:-1]).astype(F32)])
    block = jnp.arange(count, dtype=jnp.int32)
    upto = jnp.sum((targets[None, :] <= block[:, None]).astype(jnp.int32), axis=1)
    have = jnp.any(targets[None, :] == block[:, None], axis=1).astype(F32)
    return order, same, jnp.maximum(upto - 1, 0), have


def body(
    history,
    send_list,
    send_count,
    mixed_mass,
    relay_list,
    relay_target,
    mass_diag,
    mass_next,
    coupling,
    precond,
):
    devices = lax.axis_size(("dom", "sub"))
    slots = send_list.shape[2]
    values = history.shape[1]
    rows = history.shape[2]
    new_count = mass_diag.shape[0]
    picks = send_list[0]
    live = jnp.arange(slots, dtype=jnp.int32)[None, :] < send_count[0][:, None]
    outgoing = jnp.where(live[:, :, None, None], history[picks], jnp.zeros((), BF16))
    arrived = lax.all_to_all(outgoing, ("dom", "sub"), split_axis=0, concat_axis=0, tiled=True)
    mixing = mixed_mass.reshape(devices, slots, rows, rows)
    tiles = jnp.einsum("dcvs,dcsr->dcvr", arrived, mixing, preferred_element_type=F32)
    flat_tiles = tiles.reshape(devices * slots, values, rows)
    sending = flat_tiles[relay_list[0].reshape(-1)].reshape(devices, slots, values, rows)
    received = lax.all_to_all(sending, ("dom", "sub"), split_axis=0, concat_axis=0, tiled=True)
    received = received.reshape(devices * slots, values, rows)
    targets = relay_target[0].reshape(-1)
    order, same, last, have = target_order(targets, new_count)
    return mass_solve(
        order, same, last, have, coupling, received, mass_diag, mass_next, precond
    )


def solution(mesh):
    whole = ("dom", "sub")
    placed = (
        P(whole, None, None),
        P(whole, None, None),
        P(whole, None),
        P(whole, None, None),
        P(whole, None, None),
        P(whole, None, None),
        P(whole, None, None),
        P(whole, None, None),
        P(whole),
        P(whole, None, None),
    )
    return jax.shard_map(
        body,
        mesh=mesh,
        in_specs=placed,
        out_specs=(P(whole, None, None), P(whole, None, None)),
        check_vma=False,
    )
```

```python
import jax
import jax.numpy as jnp
from jax import lax
from jax.experimental import pallas as pl
from jax.experimental.pallas import tpu as pltpu
from jax.sharding import PartitionSpec as P

MESH = pl.DeviceIdType.MESH
F32 = jnp.float32
BF16 = jnp.bfloat16
STEPS = 3
CHUNK = 4
ORDER = 37
DIGITS = ((4, 32), (4, 8), (4, 2), (2, 1))


def split(value):
    high = value.astype(BF16)
    low = (value - high.astype(F32)).astype(BF16)
    return high, low


def stacked(value):
    return jnp.concatenate(split(value), axis=0)


def product(left, weights, half):
    full = jnp.dot(left, weights, preferred_element_type=F32)
    top = full[:half] + full[half:]
    width = top.shape[1] // 2
    return top[:, :width] + top[:, width:]


def solve_kernel(
    shape,
    order_ref,
    same_ref,
    last_ref,
    have_ref,
    links_ref,
    pick_ref,
    live_ref,
    relay_ref,
    hist_hbm,
    mixed_hbm,
    diag_hbm,
    next_hbm,
    prec_hbm,
    x_hbm,
    res_hbm,
    hist,
    mixed,
    out_a,
    in_a,
    out_b,
    tiles,
    stage,
    wa,
    wp,
    diag_a,
    diag_p,
    res,
    red,
    xs,
    halo,
    acc,
    trace,
    inv,
    red_src,
    red_dom,
    red_sub,
    hist_sem,
    mixed_sem,
    a_send,
    a_recv,
    b_send,
    b_recv,
    stage_sem,
    halo_send,
    halo_recv,
    link_send,
    link_recv,
    dom_send,
    dom_recv,
    sub_send,
    sub_recv,
    out_sem,
):
    doms, subs, count, values, rows, slots = shape
    devices = doms * subs
    me_dom, me_sub = lax.axis_index("dom"), lax.axis_index("sub")
    me = me_dom * subs + me_sub
    after = lax.rem(me + 1, devices)
    before = lax.rem(me + devices - 1, devices)
    after_id = (after // subs, lax.rem(after, subs))
    before_id = (before // subs, lax.rem(before, subs))

    load_hist = pltpu.make_async_copy(hist_hbm, hist, hist_sem)
    load_hist.start()
    load_mixed = pltpu.make_async_copy(mixed_hbm, mixed, mixed_sem)

    def peer_of(s):
        place = lax.rem(s * ORDER, devices)
        there = 0
        for size, stride in DIGITS:
            mine = lax.rem(me // stride, size)
            there += lax.rem(mine + lax.rem(place // stride, size), size) * stride
        return there

    def id_of(peer):
        return (peer // subs, lax.rem(peer, subs))

    barrier = pltpu.get_barrier_semaphore()

    @pl.loop(1, devices)
    def _(s):
        pl.semaphore_signal(barrier, inc=1, device_id=id_of(peer_of(s)), device_id_type=MESH)

    load_hist.wait()

    @pl.loop(0, devices)
    def _(e):
        block = hist[pick_ref[e]]
        out_a[e] = jnp.where(live_ref[e] > 0, block, jnp.zeros_like(block))

    pl.semaphore_wait(barrier, devices - 1)

    @pl.loop(1, devices)
    def _(s):
        peer = peer_of(s)
        pltpu.make_async_remote_copy(
            src_ref=out_a.at[peer],
            dst_ref=in_a.at[me],
            send_sem=a_send,
            recv_sem=a_recv,
            device_id=id_of(peer),
            device_id_type=MESH,
        ).start()

    in_a[me] = out_a[me]
    load_mixed.start()

    sources = (diag_hbm, next_hbm, prec_hbm)

    def stage_copy(chunk, which):
        slot = lax.rem(chunk, 2)
        return pltpu.make_async_copy(
            sources[which].at[pl.ds(chunk * CHUNK, CHUNK)],
            stage.at[slot, which],
            stage_sem.at[slot, which],
        )

    for which in range(3):
        stage_copy(0, which).start()
    trace[...] = jnp.zeros_like(trace)
    row = lax.broadcasted_iota(jnp.int32, (rows, rows), 0)
    col = lax.broadcasted_iota(jnp.int32, (rows, rows), 1)
    eye = row == col
    chunks = count // CHUNK

    @pl.loop(0, chunks)
    def _(chunk):
        @pl.when(chunk + 1 < chunks)
        def _():
            for which in range(3):
                stage_copy(chunk + 1, which).start()

        for which in range(3):
            stage_copy(chunk, which).wait()
        slot = lax.rem(chunk, 2)

        @pl.loop(0, CHUNK)
        def _(i):
            g = chunk * CHUNK + i
            here = stage[slot, 0, i]
            onto = stage[slot, 1, i]
            prec = stage[slot, 2, i]
            trace[...] += jnp.sum((here * prec).reshape(rows // 8, 8, rows), axis=0)
            diag_a[g] = jnp.sum(jnp.where(eye, here, 0.0), axis=0, keepdims=True)
            diag_p[g] = jnp.sum(jnp.where(eye, prec, 0.0), axis=0, keepdims=True)
            high, low = split(jnp.where(eye, 0.0, here))
            wa[g, 0:rows, 0:rows] = high
            wa[g, 0:rows, rows : 2 * rows] = low
            wrap = jnp.logical_and(g == count - 1, me == devices - 1)
            link = jnp.where(wrap, 0.0, links_ref[g].astype(F32))
            onto = onto * link
            high, low = split(onto)
            wa[g + 1, 2 * rows : 3 * rows, 0:rows] = high
            wa[g + 1, 2 * rows : 3 * rows, rows : 2 * rows] = low
            high, low = split(onto.T)
            wa[g, rows : 2 * rows, 0:rows] = high
            wa[g, rows : 2 * rows, rows : 2 * rows] = low
            high, low = split(jnp.where(eye, 0.0, prec))
            wp[g, :, 0:rows] = high
            wp[g, :, rows : 2 * rows] = low

    def reduce_over(phase, value):
        def dom_copy(peer, slot):
            return pltpu.make_async_remote_copy(
                src_ref=red_src.at[phase, 0],
                dst_ref=red_dom.at[phase, slot],
                send_sem=dom_send.at[phase, peer],
                recv_sem=dom_recv.at[phase, slot],
                device_id=(peer, me_sub),
                device_id_type=MESH,
            )

        def sub_copy(peer, slot):
            return pltpu.make_async_remote_copy(
                src_ref=red_src.at[phase, 1],
                dst_ref=red_sub.at[phase, slot],
                send_sem=sub_send.at[phase, peer],
                recv_sem=sub_recv.at[phase, slot],
                device_id=(me_dom, peer),
                device_id_type=MESH,
            )

        red_src[phase, 0] = value
        red_dom[phase, me_dom] = value

        @pl.loop(1, doms)
        def _(j):
            dom_copy(lax.rem(me_dom + j, doms), me_dom).start()

        @pl.loop(1, doms)
        def _(j):
            other = lax.rem(me_dom + j, doms)
            dom_copy(other, other).wait_recv()

        total = red_dom[phase, 0]
        for j in range(1, doms):
            total = total + red_dom[phase, j]
        red_src[phase, 1] = total
        red_sub[phase, me_sub] = total

        @pl.loop(1, subs)
        def _(j):
            sub_copy(lax.rem(me_sub + j, subs), me_sub).start()

        @pl.loop(1, subs)
        def _(j):
            other = lax.rem(me_sub + j, subs)
            sub_copy(other, other).wait_recv()

        total = red_sub[phase, 0]
        for j in range(1, subs):
            total = total + red_sub[phase, j]

        @pl.loop(1, doms)
        def _(j):
            dom_copy(lax.rem(me_dom + j, doms), me_dom).wait_send()

        @pl.loop(1, subs)
        def _(j):
            sub_copy(lax.rem(me_sub + j, subs), me_sub).wait_send()

        return total

    link_copy = pltpu.make_async_remote_copy(
        src_ref=wa.at[count, pl.ds(2 * rows, rows)],
        dst_ref=wa.at[0, pl.ds(2 * rows, rows)],
        send_sem=link_send,
        recv_sem=link_recv,
        device_id=after_id,
        device_id_type=MESH,
    )
    link_copy.start()
    theta = reduce_over(0, trace[...])
    theta = jnp.sum(jnp.sum(theta, axis=0, keepdims=True), axis=1, keepdims=True)
    inv[...] = jnp.broadcast_to((1.0 * devices * count * rows) / theta, inv.shape)

    others = pl.ds(0, devices - 1)
    load_mixed.wait()
    pltpu.make_async_copy(in_a.at[others], in_a.at[others], a_recv).wait()

    def mixed_tile(peer):
        spot = relay_ref[peer]
        return jnp.dot(in_a[spot], mixed[spot], preferred_element_type=F32)

    def send_tile(s):
        peer = peer_of(s)
        pltpu.make_async_remote_copy(
            src_ref=out_b.at[peer],
            dst_ref=tiles.at[me],
            send_sem=b_send,
            recv_sem=b_recv,
            device_id=id_of(peer),
            device_id_type=MESH,
        ).start()

    @pl.loop(1, devices)
    def _(s):
        peer = peer_of(s)
        out_b[peer] = mixed_tile(peer)

        @pl.when(s > 1)
        def _():
            send_tile(s - 1)

    tiles[me] = mixed_tile(me)
    send_tile(devices - 1)
    pltpu.make_async_copy(out_a.at[others], out_a.at[others], a_send).wait()
    pltpu.make_async_copy(out_b.at[others], out_b.at[others], b_send).wait()
    pltpu.make_async_copy(tiles.at[others], tiles.at[others], b_recv).wait()


    def add_tile(j, running):
        running = running * same_ref[j] + tiles[order_ref[j]]
        red[j] = running
        return running

    lax.fori_loop(0, slots, add_tile, jnp.zeros((values, rows), F32))

    @pl.loop(0, count)
    def _(g):
        res[0, g] = red[last_ref[g]] * have_ref[g]

    def precondition(g, k, value):
        out = product(stacked(value), wp[g], values) + value * diag_p[g]
        red[k * count + g] = out
        xs[k % 2, g + 1] = stacked(out)

    def apply_block(g, k, left, right):
        here = xs[k % 2, g + 1]
        image = product(jnp.concatenate([here, right, left], axis=1), wa[g], values)
        field = red[k * count + g]
        image = image + field * diag_a[g]
        now = res[k, g]
        later = now - image * inv[0:1]
        res[k + 1, g] = later
        step = now - later
        if k == 0:
            acc[0] += field * step
        if k == 1:
            acc[1] += field * (res[0, g] - now)
            acc[2] += field * step
        if k == 2:
            acc[3] += field * (res[1, g] - now)
            acc[4] += field * step
            acc[5] += red[g] * later
            acc[6] += red[count + g] * later
            acc[7] += field * later
        if k + 1 < STEPS:
            precondition(g, k + 1, later)

    def inner(g, k):
        apply_block(g, k, xs[k % 2, g], xs[k % 2, g + 2])

    def halo_copy(k, side):
        return pltpu.make_async_remote_copy(
            src_ref=xs.at[k % 2, count if side == 0 else 1],
            dst_ref=halo.at[k, side],
            send_sem=halo_send.at[k, side],
            recv_sem=halo_recv.at[k, side],
            device_id=after_id if side == 0 else before_id,
            device_id_type=MESH,
        )

    middle = count // 2
    acc[...] = jnp.zeros_like(acc)
    precondition(0, 0, res[0, 0])
    precondition(count - 1, 0, res[0, count - 1])

    @pl.loop(1, 9)
    def _(g):
        precondition(g, 0, res[0, g])

    halo_copy(0, 0).start()
    halo_copy(0, 1).start()

    @pl.loop(9, count - 1)
    def _(g):
        precondition(g, 0, res[0, g])

    link_copy.wait()
    for k in range(STEPS):

        @pl.loop(1, middle)
        def _(g):
            inner(g, k)

        halo_copy(k, 0).wait()
        halo_copy(k, 1).wait()
        apply_block(0, k, halo[k, 0], xs[k % 2, 2])
        apply_block(count - 1, k, xs[k % 2, count - 1], halo[k, 1])

        @pl.loop(middle, middle + 4)
        def _(g):
            inner(g, k)

        if k + 1 < STEPS:
            halo_copy(k + 1, 0).start()
            halo_copy(k + 1, 1).start()

        @pl.loop(middle + 4, count - 1)
        def _(g):
            inner(g, k)

    lane = lax.broadcasted_iota(jnp.int32, (values, rows), 1)
    packed = jnp.zeros((values, rows), F32)
    for j in range(8):
        packed = packed + jnp.where(lane == j, jnp.sum(acc[j], axis=1, keepdims=True), 0.0)
    packed = jnp.concatenate([packed, jnp.zeros((rows - values, rows), F32)], axis=0)
    total = reduce_over(1, packed.T[0:8])

    def over(top, bottom):
        usable = bottom != 0.0
        return jnp.where(usable, top / jnp.where(usable, bottom, 1.0), 0.0)

    g00, g10, g11, g21, g22 = (total[j : j + 1] for j in range(5))
    h0, h1, h2 = (-total[j : j + 1] for j in range(5, 8))
    l1, l2 = over(g10, g00), over(g11, g00)
    d1 = g11 - l1 * g10
    mix = g21 - l2 * g10
    l3 = over(mix, d1)
    d2 = g22 - l2 * g11 - l3 * mix
    y1 = h1 - l1 * h0
    y2 = h2 - l2 * h0 - l3 * y1
    e2 = over(y2, d2)
    e1 = over(y1, d1) - l3 * e2
    e0 = over(h0, g00) - l1 * e1 - l2 * e2
    weights = jnp.concatenate([e0, e1, e2, jnp.zeros((rows - 3, rows), F32)], axis=0).T
    e0 = jnp.broadcast_to(weights[0:values, 0:1], (values, rows))
    e1 = jnp.broadcast_to(weights[0:values, 1:2], (values, rows))
    e2 = jnp.broadcast_to(weights[0:values, 2:3], (values, rows))
    scale = inv[0:1]
    x0, x1, x2 = (1.0 - e0) * scale, (1.0 - e1) * scale, (1.0 - e2) * scale
    r1, r2, r3 = e1 - e0, e2 - e1, 1.0 - e2

    @pl.loop(0, count)
    def _(g):
        u0, u1, u2 = red[g], red[count + g], red[2 * count + g]
        red[g] = x0 * u0 + x1 * u1 + x2 * u2
        res[0, g] = e0 * res[0, g] + r1 * res[1, g] + r2 * res[2, g] + r3 * res[3, g]

    put_x = pltpu.make_async_copy(red.at[pl.ds(0, count)], x_hbm, out_sem.at[0])
    put_r = pltpu.make_async_copy(res.at[0], res_hbm, out_sem.at[1])
    put_x.start()
    put_r.start()
    put_x.wait()
    put_r.wait()


def mass_solve(order, same, last, have, links, pick, live, relay, history, mixed, mass_diag, mass_next, precond):
    doms, subs = lax.axis_size("dom"), lax.axis_size("sub")
    slots = mixed.shape[0]
    blocks, values, rows = history.shape
    count = mass_diag.shape[0]
    shape = (doms, subs, count, values, rows, slots)

    def kernel(*refs):
        solve_kernel(shape, *refs)

    smem = pl.BlockSpec(memory_space=pltpu.SMEM)
    hbm = pl.BlockSpec(memory_space=pl.ANY)
    field = jax.ShapeDtypeStruct((count, values, rows), F32)
    dma = pltpu.SemaphoreType.DMA
    return pl.pallas_call(
        kernel,
        out_shape=(field, field),
        in_specs=[smem] * 8 + [hbm] * 5,
        out_specs=(hbm, hbm),
        scratch_shapes=[
            pltpu.VMEM((blocks, values, rows), BF16),
            pltpu.VMEM((slots, rows, rows), BF16),
            pltpu.VMEM((slots, values, rows), BF16),
            pltpu.VMEM((slots, values, rows), BF16),
            pltpu.VMEM((slots, values, rows), F32),
            pltpu.VMEM((slots, values, rows), F32),
            pltpu.VMEM((2, 3, CHUNK, rows, rows), F32),
            pltpu.VMEM((count + 1, 3 * rows, 2 * rows), BF16),
            pltpu.VMEM((count, rows, 2 * rows), BF16),
            pltpu.VMEM((count, 1, rows), F32),
            pltpu.VMEM((count, 1, rows), F32),
            pltpu.VMEM((STEPS + 1, count, values, rows), F32),
            pltpu.VMEM((STEPS * count, values, rows), F32),
            pltpu.VMEM((2, count + 2, 2 * values, rows), BF16),
            pltpu.VMEM((STEPS, 2, 2 * values, rows), BF16),
            pltpu.VMEM((8, values, rows), F32),
            pltpu.VMEM((8, rows), F32),
            pltpu.VMEM((8, rows), F32),
            pltpu.VMEM((2, 2, 8, rows), F32),
            pltpu.VMEM((2, doms, 8, rows), F32),
            pltpu.VMEM((2, subs, 8, rows), F32),
            dma,
            dma,
            dma,
            dma,
            dma,
            dma,
            dma((2, 3)),
            dma((STEPS, 2)),
            dma((STEPS, 2)),
            dma,
            dma,
            dma((2, doms)),
            dma((2, doms)),
            dma((2, subs)),
            dma((2, subs)),
            dma((2,)),
        ],
        compiler_params=pltpu.CompilerParams(
            collective_id=0, has_side_effects=True, vmem_limit_bytes=60 * 1024 * 1024
        ),
    )(order, same, last, have, links, pick, live, relay, history, mixed, mass_diag, mass_next, precond)


def target_order(targets, count):
    slots = targets.shape[0]
    spot = jnp.arange(slots, dtype=jnp.int32)
    key = targets * slots + spot
    rank = jnp.sum((key[None, :] < key[:, None]).astype(jnp.int32), axis=1)
    at = rank[None, :] == spot[:, None]
    order = jnp.sum(jnp.where(at, spot[None, :], 0), axis=1)
    ordered = jnp.sum(jnp.where(at, targets[None, :], 0), axis=1)
    same = jnp.concatenate([jnp.zeros((1,), F32), (ordered[1:] == ordered[:-1]).astype(F32)])
    block = jnp.arange(count, dtype=jnp.int32)
    upto = jnp.sum((targets[None, :] <= block[:, None]).astype(jnp.int32), axis=1)
    have = jnp.any(targets[None, :] == block[:, None], axis=1).astype(F32)
    return order, same, jnp.maximum(upto - 1, 0), have


def body(
    history,
    send_list,
    send_count,
    mixed_mass,
    relay_list,
    relay_target,
    mass_diag,
    mass_next,
    coupling,
    precond,
):
    new_count = mass_diag.shape[0]
    targets = relay_target.reshape(-1)
    order, same, last, have = target_order(targets, new_count)
    return mass_solve(
        order,
        same,
        last,
        have,
        coupling,
        send_list.reshape(-1),
        send_count.reshape(-1),
        relay_list.reshape(-1),
        history,
        mixed_mass,
        mass_diag,
        mass_next,
        precond,
    )


def solution(mesh):
    whole = ("dom", "sub")
    placed = (
        P(whole, None, None),
        P(whole, None, None),
        P(whole, None),
        P(whole, None, None),
        P(whole, None, None),
        P(whole, None, None),
        P(whole, None, None),
        P(whole, None, None),
        P(whole),
        P(whole, None, None),
    )
    return jax.shard_map(
        body,
        mesh=mesh,
        in_specs=placed,
        out_specs=(P(whole, None, None), P(whole, None, None)),
        check_vma=False,
    )
```

```python
import jax
import jax.numpy as jnp
from jax import lax
from jax.experimental import pallas as pl
from jax.experimental.pallas import tpu as pltpu
from jax.sharding import PartitionSpec as P

MESH = pl.DeviceIdType.MESH
F32 = jnp.float32
BF16 = jnp.bfloat16
STEPS = 3
CHUNK = 4
ORDER = 37
FIRST_BITS = 0b0101010


def split(value):
    high = value.astype(BF16)
    low = (value - high.astype(F32)).astype(BF16)
    return high, low


def stacked(value):
    return jnp.concatenate(split(value), axis=0)


def product(left, weights, half):
    full = jnp.dot(left, weights, preferred_element_type=F32)
    top = full[:half] + full[half:]
    width = top.shape[1] // 2
    return top[:, :width] + top[:, width:]


def solve_kernel(
    shape,
    order_ref,
    same_ref,
    last_ref,
    have_ref,
    links_ref,
    pick_ref,
    live_ref,
    relay_ref,
    hist_hbm,
    mixed_hbm,
    diag_hbm,
    next_hbm,
    prec_hbm,
    x_hbm,
    res_hbm,
    hist,
    mixed,
    out_a,
    in_a,
    out_b,
    tiles,
    stage,
    wa,
    wp,
    diag_a,
    diag_p,
    res,
    red,
    xs,
    halo,
    acc,
    trace,
    inv,
    red_src,
    red_dom,
    red_sub,
    enter,
    hist_sem,
    mixed_sem,
    a_send,
    a_recv,
    b_send,
    b_recv,
    stage_sem,
    halo_send,
    halo_recv,
    link_send,
    link_recv,
    dom_send,
    dom_recv,
    sub_send,
    sub_recv,
    out_sem,
):
    doms, subs, count, values, rows, slots = shape
    devices = doms * subs
    me_dom, me_sub = lax.axis_index("dom"), lax.axis_index("sub")
    me = me_dom * subs + me_sub
    after = lax.rem(me + 1, devices)
    before = lax.rem(me + devices - 1, devices)
    after_id = (after // subs, lax.rem(after, subs))
    before_id = (before // subs, lax.rem(before, subs))

    load_hist = pltpu.make_async_copy(hist_hbm, hist, hist_sem)
    load_hist.start()
    load_mixed = pltpu.make_async_copy(mixed_hbm, mixed, mixed_sem)

    def peer_of(s):
        place = (s * ORDER) & (devices - 1)
        carry = (place & me & FIRST_BITS) << 1
        return place ^ me ^ carry

    def id_of(peer):
        return (peer >> 3, peer & (subs - 1))

    width = 4
    me_y, me_x = me_dom >> 2, me_dom & (width - 1)

    def line_x(j):
        return (me_y * width + ((me_x + j) & (width - 1)), me_sub)

    def line_y(j):
        return (((me_y + j) & (width - 1)) * width + me_x, me_sub)

    barrier = pltpu.get_barrier_semaphore()
    for j in range(1, subs):
        other = (me_dom, (me_sub + j) & (subs - 1))
        pl.semaphore_signal(barrier, inc=1, device_id=other, device_id_type=MESH)
    for j in range(1, width):
        pl.semaphore_signal(barrier, inc=1, device_id=line_x(j), device_id_type=MESH)
        pl.semaphore_signal(barrier, inc=1, device_id=line_y(j), device_id_type=MESH)

    load_hist.wait()

    @pl.loop(0, devices)
    def _(e):
        block = hist[pick_ref[e]]
        out_a[e] = jnp.where(live_ref[e] > 0, block, jnp.zeros_like(block))

    pl.semaphore_wait(barrier, subs - 1 + 2 * (width - 1))
    for j in range(1, width):
        pl.semaphore_signal(enter.at[0], inc=1, device_id=line_x(j), device_id_type=MESH)
    pl.semaphore_wait(enter.at[0], width - 1)
    for j in range(1, width):
        pl.semaphore_signal(enter.at[1], inc=1, device_id=line_y(j), device_id_type=MESH)
    pl.semaphore_wait(enter.at[1], width - 1)

    @pl.loop(1, devices)
    def _(s):
        peer = peer_of(s)
        pltpu.make_async_remote_copy(
            src_ref=out_a.at[peer],
            dst_ref=in_a.at[me],
            send_sem=a_send,
            recv_sem=a_recv,
            device_id=id_of(peer),
            device_id_type=MESH,
        ).start()

    in_a[me] = out_a[me]
    load_mixed.start()

    sources = (diag_hbm, next_hbm, prec_hbm)

    def stage_copy(chunk, which):
        slot = lax.rem(chunk, 2)
        return pltpu.make_async_copy(
            sources[which].at[pl.ds(chunk * CHUNK, CHUNK)],
            stage.at[slot, which],
            stage_sem.at[slot, which],
        )

    for which in range(3):
        stage_copy(0, which).start()
    trace[...] = jnp.zeros_like(trace)
    row = lax.broadcasted_iota(jnp.int32, (rows, rows), 0)
    col = lax.broadcasted_iota(jnp.int32, (rows, rows), 1)
    eye = row == col
    chunks = count // CHUNK

    @pl.loop(0, chunks)
    def _(chunk):
        @pl.when(chunk + 1 < chunks)
        def _():
            for which in range(3):
                stage_copy(chunk + 1, which).start()

        for which in range(3):
            stage_copy(chunk, which).wait()
        slot = lax.rem(chunk, 2)

        @pl.loop(0, CHUNK)
        def _(i):
            g = chunk * CHUNK + i
            here = stage[slot, 0, i]
            onto = stage[slot, 1, i]
            prec = stage[slot, 2, i]
            trace[...] += jnp.sum((here * prec).reshape(rows // 8, 8, rows), axis=0)
            diag_a[g] = jnp.sum(jnp.where(eye, here, 0.0), axis=0, keepdims=True)
            diag_p[g] = jnp.sum(jnp.where(eye, prec, 0.0), axis=0, keepdims=True)
            high, low = split(jnp.where(eye, 0.0, here))
            wa[g, 0:rows, 0:rows] = high
            wa[g, 0:rows, rows : 2 * rows] = low
            wrap = jnp.logical_and(g == count - 1, me == devices - 1)
            link = jnp.where(wrap, 0.0, links_ref[g].astype(F32))
            onto = onto * link
            high, low = split(onto)
            wa[g + 1, 2 * rows : 3 * rows, 0:rows] = high
            wa[g + 1, 2 * rows : 3 * rows, rows : 2 * rows] = low
            high, low = split(onto.T)
            wa[g, rows : 2 * rows, 0:rows] = high
            wa[g, rows : 2 * rows, rows : 2 * rows] = low
            high, low = split(jnp.where(eye, 0.0, prec))
            wp[g, :, 0:rows] = high
            wp[g, :, rows : 2 * rows] = low

    def reduce_over(phase, value):
        def dom_copy(peer, slot):
            return pltpu.make_async_remote_copy(
                src_ref=red_src.at[phase, 0],
                dst_ref=red_dom.at[phase, slot],
                send_sem=dom_send.at[phase, peer],
                recv_sem=dom_recv.at[phase, slot],
                device_id=(peer, me_sub),
                device_id_type=MESH,
            )

        def sub_copy(peer, slot):
            return pltpu.make_async_remote_copy(
                src_ref=red_src.at[phase, 1],
                dst_ref=red_sub.at[phase, slot],
                send_sem=sub_send.at[phase, peer],
                recv_sem=sub_recv.at[phase, slot],
                device_id=(me_dom, peer),
                device_id_type=MESH,
            )

        red_src[phase, 0] = value
        red_dom[phase, me_dom] = value

        @pl.loop(1, doms)
        def _(j):
            dom_copy(lax.rem(me_dom + j, doms), me_dom).start()

        @pl.loop(1, doms)
        def _(j):
            other = lax.rem(me_dom + j, doms)
            dom_copy(other, other).wait_recv()

        total = red_dom[phase, 0]
        for j in range(1, doms):
            total = total + red_dom[phase, j]
        red_src[phase, 1] = total
        red_sub[phase, me_sub] = total

        @pl.loop(1, subs)
        def _(j):
            sub_copy(lax.rem(me_sub + j, subs), me_sub).start()

        @pl.loop(1, subs)
        def _(j):
            other = lax.rem(me_sub + j, subs)
            sub_copy(other, other).wait_recv()

        total = red_sub[phase, 0]
        for j in range(1, subs):
            total = total + red_sub[phase, j]

        @pl.loop(1, doms)
        def _(j):
            dom_copy(lax.rem(me_dom + j, doms), me_dom).wait_send()

        @pl.loop(1, subs)
        def _(j):
            sub_copy(lax.rem(me_sub + j, subs), me_sub).wait_send()

        return total

    link_copy = pltpu.make_async_remote_copy(
        src_ref=wa.at[count, pl.ds(2 * rows, rows)],
        dst_ref=wa.at[0, pl.ds(2 * rows, rows)],
        send_sem=link_send,
        recv_sem=link_recv,
        device_id=after_id,
        device_id_type=MESH,
    )
    link_copy.start()
    theta = reduce_over(0, trace[...])
    theta = jnp.sum(jnp.sum(theta, axis=0, keepdims=True), axis=1, keepdims=True)
    inv[...] = jnp.broadcast_to((1.0 * devices * count * rows) / theta, inv.shape)

    others = pl.ds(0, devices - 1)
    load_mixed.wait()
    pltpu.make_async_copy(in_a.at[others], in_a.at[others], a_recv).wait()

    def mixed_tile(peer):
        spot = relay_ref[peer]
        return jnp.dot(in_a[spot], mixed[spot], preferred_element_type=F32)

    def send_tile(peer):
        pltpu.make_async_remote_copy(
            src_ref=out_b.at[peer],
            dst_ref=tiles.at[me],
            send_sem=b_send,
            recv_sem=b_recv,
            device_id=id_of(peer),
            device_id_type=MESH,
        ).start()

    first = peer_of(1)
    out_b[first] = mixed_tile(first)

    def next_tile(s, ready):
        peer = peer_of(s)
        out_b[peer] = mixed_tile(peer)
        send_tile(ready)
        return peer

    ready = lax.fori_loop(2, devices, next_tile, first)
    tiles[me] = mixed_tile(me)
    send_tile(ready)
    pltpu.make_async_copy(out_a.at[others], out_a.at[others], a_send).wait()
    pltpu.make_async_copy(out_b.at[others], out_b.at[others], b_send).wait()
    pltpu.make_async_copy(tiles.at[others], tiles.at[others], b_recv).wait()


    def add_tile(j, running):
        running = running * same_ref[j] + tiles[order_ref[j]]
        red[j] = running
        return running

    lax.fori_loop(0, slots, add_tile, jnp.zeros((values, rows), F32))

    @pl.loop(0, count)
    def _(g):
        res[0, g] = red[last_ref[g]] * have_ref[g]

    def precondition(blocks, k, fields):
        outs = [
            product(stacked(field), wp[g], values) + field * diag_p[g]
            for g, field in zip(blocks, fields)
        ]
        for g, out in zip(blocks, outs):
            red[k * count + g] = out
            xs[k % 2, g + 1] = stacked(out)

    def apply_blocks(blocks, k, operands):
        fields = [red[k * count + g] for g in blocks]
        nows = [res[k, g] for g in blocks]
        befores = [res[k - 1, g] for g in blocks] if k > 0 else None
        images = [
            product(operand, wa[g], values) + field * diag_a[g]
            for g, field, operand in zip(blocks, fields, operands)
        ]
        laters = [now - image * inv[0:1] for now, image in zip(nows, images)]
        steps = [now - later for now, later in zip(nows, laters)]

        def dots(slot, left, right):
            acc[slot] += sum(a * b for a, b in zip(left, right))

        if k + 1 < STEPS:
            precondition(blocks, k + 1, laters)
        for g, later in zip(blocks, laters):
            res[k + 1, g] = later
        if k == 0:
            dots(0, fields, steps)
        else:
            dots(2 * k - 1, fields, [x - y for x, y in zip(befores, nows)])
            dots(2 * k, fields, steps)
        if k == 2:
            dots(5, [red[g] for g in blocks], laters)
            dots(6, [red[count + g] for g in blocks], laters)
            dots(7, fields, laters)

    def inner(g, k):
        near = [xs[k % 2, g + i] for i in range(4)]
        apply_blocks(
            (g, g + 1), k, [jnp.concatenate([near[i + 1], near[i + 2], near[i]], axis=1) for i in range(2)]
        )

    def inners(start, stop, k):
        @pl.loop(0, (stop - start) // 2)
        def _(i):
            inner(start + 2 * i, k)

    def preconditions(start, stop):
        @pl.loop(0, (stop - start) // 2)
        def _(i):
            g = start + 2 * i
            precondition((g, g + 1), 0, (res[0, g], res[0, g + 1]))

    def halo_copy(k, side):
        return pltpu.make_async_remote_copy(
            src_ref=xs.at[k % 2, count if side == 0 else 1],
            dst_ref=halo.at[k, side],
            send_sem=halo_send.at[k, side],
            recv_sem=halo_recv.at[k, side],
            device_id=after_id if side == 0 else before_id,
            device_id_type=MESH,
        )

    edges = (0, count - 1)
    middle = count // 2 + 1
    acc[...] = jnp.zeros_like(acc)
    precondition(edges, 0, [res[0, g] for g in edges])
    preconditions(1, 9)
    halo_copy(0, 0).start()
    halo_copy(0, 1).start()
    preconditions(9, count - 1)

    link_copy.wait()
    for k in range(STEPS):
        inners(1, middle, k)
        halo_copy(k, 0).wait()
        halo_copy(k, 1).wait()
        buf = k % 2
        apply_blocks(
            edges,
            k,
            [
                jnp.concatenate([xs[buf, 1], xs[buf, 2], halo[k, 0]], axis=1),
                jnp.concatenate([xs[buf, count], halo[k, 1], xs[buf, count - 1]], axis=1),
            ],
        )
        inners(middle, middle + 4, k)
        if k + 1 < STEPS:
            halo_copy(k + 1, 0).start()
            halo_copy(k + 1, 1).start()
        inners(middle + 4, count - 1, k)

    lane = lax.broadcasted_iota(jnp.int32, (values, rows), 1)
    packed = jnp.zeros((values, rows), F32)
    for j in range(8):
        packed = packed + jnp.where(lane == j, jnp.sum(acc[j], axis=1, keepdims=True), 0.0)
    packed = jnp.concatenate([packed, jnp.zeros((rows - values, rows), F32)], axis=0)
    total = reduce_over(1, packed.T[0:8])

    def over(top, bottom):
        usable = bottom != 0.0
        return jnp.where(usable, top / jnp.where(usable, bottom, 1.0), 0.0)

    g00, g10, g11, g21, g22 = (total[j : j + 1] for j in range(5))
    h0, h1, h2 = (-total[j : j + 1] for j in range(5, 8))
    l1, l2 = over(g10, g00), over(g11, g00)
    d1 = g11 - l1 * g10
    mix = g21 - l2 * g10
    l3 = over(mix, d1)
    d2 = g22 - l2 * g11 - l3 * mix
    y1 = h1 - l1 * h0
    y2 = h2 - l2 * h0 - l3 * y1
    e2 = over(y2, d2)
    e1 = over(y1, d1) - l3 * e2
    e0 = over(h0, g00) - l1 * e1 - l2 * e2
    weights = jnp.concatenate([e0, e1, e2, jnp.zeros((rows - 3, rows), F32)], axis=0).T
    e0 = jnp.broadcast_to(weights[0:values, 0:1], (values, rows))
    e1 = jnp.broadcast_to(weights[0:values, 1:2], (values, rows))
    e2 = jnp.broadcast_to(weights[0:values, 2:3], (values, rows))
    scale = inv[0:1]
    x0, x1, x2 = (1.0 - e0) * scale, (1.0 - e1) * scale, (1.0 - e2) * scale
    r1, r2, r3 = e1 - e0, e2 - e1, 1.0 - e2

    @pl.loop(0, count)
    def _(g):
        u0, u1, u2 = red[g], red[count + g], red[2 * count + g]
        red[g] = x0 * u0 + x1 * u1 + x2 * u2
        res[0, g] = e0 * res[0, g] + r1 * res[1, g] + r2 * res[2, g] + r3 * res[3, g]

    put_x = pltpu.make_async_copy(red.at[pl.ds(0, count)], x_hbm, out_sem.at[0])
    put_r = pltpu.make_async_copy(res.at[0], res_hbm, out_sem.at[1])
    put_x.start()
    put_r.start()
    put_x.wait()
    put_r.wait()


def mass_solve(order, same, last, have, links, pick, live, relay, history, mixed, mass_diag, mass_next, precond):
    doms, subs = lax.axis_size("dom"), lax.axis_size("sub")
    slots = mixed.shape[0]
    blocks, values, rows = history.shape
    count = mass_diag.shape[0]
    shape = (doms, subs, count, values, rows, slots)

    def kernel(*refs):
        solve_kernel(shape, *refs)

    smem = pl.BlockSpec(memory_space=pltpu.SMEM)
    hbm = pl.BlockSpec(memory_space=pl.ANY)
    field = jax.ShapeDtypeStruct((count, values, rows), F32)
    dma = pltpu.SemaphoreType.DMA
    return pl.pallas_call(
        kernel,
        out_shape=(field, field),
        in_specs=[smem] * 8 + [hbm] * 5,
        out_specs=(hbm, hbm),
        scratch_shapes=[
            pltpu.VMEM((blocks, values, rows), BF16),
            pltpu.VMEM((slots, rows, rows), BF16),
            pltpu.VMEM((slots, values, rows), BF16),
            pltpu.VMEM((slots, values, rows), BF16),
            pltpu.VMEM((slots, values, rows), F32),
            pltpu.VMEM((slots, values, rows), F32),
            pltpu.VMEM((2, 3, CHUNK, rows, rows), F32),
            pltpu.VMEM((count + 1, 3 * rows, 2 * rows), BF16),
            pltpu.VMEM((count, rows, 2 * rows), BF16),
            pltpu.VMEM((count, 1, rows), F32),
            pltpu.VMEM((count, 1, rows), F32),
            pltpu.VMEM((STEPS + 1, count, values, rows), F32),
            pltpu.VMEM((STEPS * count, values, rows), F32),
            pltpu.VMEM((2, count + 2, 2 * values, rows), BF16),
            pltpu.VMEM((STEPS, 2, 2 * values, rows), BF16),
            pltpu.VMEM((8, values, rows), F32),
            pltpu.VMEM((8, rows), F32),
            pltpu.VMEM((8, rows), F32),
            pltpu.VMEM((2, 2, 8, rows), F32),
            pltpu.VMEM((2, doms, 8, rows), F32),
            pltpu.VMEM((2, subs, 8, rows), F32),
            pltpu.SemaphoreType.REGULAR((2,)),
            dma,
            dma,
            dma,
            dma,
            dma,
            dma,
            dma((2, 3)),
            dma((STEPS, 2)),
            dma((STEPS, 2)),
            dma,
            dma,
            dma((2, doms)),
            dma((2, doms)),
            dma((2, subs)),
            dma((2, subs)),
            dma((2,)),
        ],
        compiler_params=pltpu.CompilerParams(
            collective_id=0, has_side_effects=True, vmem_limit_bytes=60 * 1024 * 1024
        ),
    )(order, same, last, have, links, pick, live, relay, history, mixed, mass_diag, mass_next, precond)


def target_order(targets, count):
    slots = targets.shape[0]
    spot = jnp.arange(slots, dtype=jnp.int32)
    key = targets * slots + spot
    rank = jnp.sum((key[None, :] < key[:, None]).astype(jnp.int32), axis=1)
    at = rank[None, :] == spot[:, None]
    order = jnp.sum(jnp.where(at, spot[None, :], 0), axis=1)
    ordered = jnp.sum(jnp.where(at, targets[None, :], 0), axis=1)
    same = jnp.concatenate([jnp.zeros((1,), F32), (ordered[1:] == ordered[:-1]).astype(F32)])
    block = jnp.arange(count, dtype=jnp.int32)
    upto = jnp.sum((targets[None, :] <= block[:, None]).astype(jnp.int32), axis=1)
    have = jnp.any(targets[None, :] == block[:, None], axis=1).astype(F32)
    return order, same, jnp.maximum(upto - 1, 0), have


def body(
    history,
    send_list,
    send_count,
    mixed_mass,
    relay_list,
    relay_target,
    mass_diag,
    mass_next,
    coupling,
    precond,
):
    new_count = mass_diag.shape[0]
    targets = relay_target.reshape(-1)
    order, same, last, have = target_order(targets, new_count)
    return mass_solve(
        order,
        same,
        last,
        have,
        coupling,
        send_list.reshape(-1),
        send_count.reshape(-1),
        relay_list.reshape(-1),
        history,
        mixed_mass,
        mass_diag,
        mass_next,
        precond,
    )


def solution(mesh):
    whole = ("dom", "sub")
    placed = (
        P(whole, None, None),
        P(whole, None, None),
        P(whole, None),
        P(whole, None, None),
        P(whole, None, None),
        P(whole, None, None),
        P(whole, None, None),
        P(whole, None, None),
        P(whole),
        P(whole, None, None),
    )
    return jax.shard_map(
        body,
        mesh=mesh,
        in_specs=placed,
        out_specs=(P(whole, None, None), P(whole, None, None)),
        check_vma=False,
    )
```

```python
import jax
import jax.numpy as jnp
from jax import lax
from jax.experimental import pallas as pl
from jax.experimental.pallas import tpu as pltpu
from jax.sharding import PartitionSpec as P

MESH = pl.DeviceIdType.MESH
F32 = jnp.float32
BF16 = jnp.bfloat16
STEPS = 3
CHUNK = 4
ORDER = 37
GROUP = 4
BATCH = 8
LEVELS = 32767.0
FIRST_BITS = 0b0101010


def split(value):
    high = value.astype(BF16)
    low = (value - high.astype(F32)).astype(BF16)
    return high, low


def stacked(value):
    return jnp.concatenate(split(value), axis=0)


def product(left, weights, half):
    full = jnp.dot(left, weights, preferred_element_type=F32)
    top = full[:half] + full[half:]
    width = top.shape[1] // 2
    return top[:, :width] + top[:, width:]


def solve_kernel(
    shape,
    target_ref,
    links_ref,
    pick_ref,
    live_ref,
    relay_ref,
    hist_hbm,
    mixed_hbm,
    diag_hbm,
    next_hbm,
    prec_hbm,
    x_hbm,
    res_hbm,
    hist,
    mixed,
    out_a,
    in_a,
    out_b,
    tiles,
    unit_out,
    unit_in,
    stage,
    wa,
    wp,
    diag_a,
    diag_p,
    res,
    red,
    xs,
    halo,
    acc,
    trace,
    inv,
    red_src,
    red_dom,
    red_sub,
    rank_rows,
    table,
    table_sem,
    enter,
    hist_sem,
    mixed_sem,
    a_send,
    a_recv,
    b_send,
    b_recv,
    c_send,
    c_recv,
    stage_sem,
    halo_send,
    halo_recv,
    link_send,
    link_recv,
    dom_send,
    dom_recv,
    sub_send,
    sub_recv,
    out_sem,
):
    doms, subs, count, values, rows, slots = shape
    devices = doms * subs
    me_dom, me_sub = lax.axis_index("dom"), lax.axis_index("sub")
    me = me_dom * subs + me_sub
    after = lax.rem(me + 1, devices)
    before = lax.rem(me + devices - 1, devices)
    after_id = (after // subs, lax.rem(after, subs))
    before_id = (before // subs, lax.rem(before, subs))

    load_hist = pltpu.make_async_copy(hist_hbm, hist, hist_sem)
    load_hist.start()
    load_mixed = pltpu.make_async_copy(mixed_hbm, mixed, mixed_sem)

    def peer_of(s):
        place = (s * ORDER) & (devices - 1)
        carry = (place & me & FIRST_BITS) << 1
        return place ^ me ^ carry

    def id_of(peer):
        return (peer >> 3, peer & (subs - 1))

    width = 4
    me_y, me_x = me_dom >> 2, me_dom & (width - 1)

    def line_x(j):
        return (me_y * width + ((me_x + j) & (width - 1)), me_sub)

    def line_y(j):
        return (((me_y + j) & (width - 1)) * width + me_x, me_sub)

    barrier = pltpu.get_barrier_semaphore()
    for j in range(1, subs):
        other = (me_dom, (me_sub + j) & (subs - 1))
        pl.semaphore_signal(barrier, inc=1, device_id=other, device_id_type=MESH)
    for j in range(1, width):
        pl.semaphore_signal(barrier, inc=1, device_id=line_x(j), device_id_type=MESH)
        pl.semaphore_signal(barrier, inc=1, device_id=line_y(j), device_id_type=MESH)

    pl.semaphore_wait(barrier, subs - 1 + 2 * (width - 1))
    for j in range(1, width):
        pl.semaphore_signal(enter.at[0], inc=1, device_id=line_x(j), device_id_type=MESH)
    pl.semaphore_wait(enter.at[0], width - 1)
    for j in range(1, width):
        pl.semaphore_signal(enter.at[1], inc=1, device_id=line_y(j), device_id_type=MESH)

    load_hist.wait()

    @pl.loop(0, devices)
    def _(e):
        block = hist[pick_ref[e]]
        out_a[e] = jnp.where(live_ref[e] > 0, block, jnp.zeros_like(block))

    pl.semaphore_wait(enter.at[1], width - 1)

    @pl.loop(1, devices)
    def _(s):
        peer = peer_of(s)
        pltpu.make_async_remote_copy(
            src_ref=out_a.at[peer],
            dst_ref=in_a.at[me],
            send_sem=a_send,
            recv_sem=a_recv,
            device_id=id_of(peer),
            device_id_type=MESH,
        ).start()

    in_a[me] = out_a[me]
    load_mixed.start()

    spot = lax.broadcasted_iota(jnp.int32, (slots, slots), 0)
    place = lax.broadcasted_iota(jnp.int32, (slots, slots), 1)
    target = jnp.broadcast_to(target_ref[...], (slots, slots))
    target_of = jnp.sum(jnp.where(spot == place, target, 0), axis=1, keepdims=True)
    earlier = target * slots + place < target_of * slots + spot
    rank = jnp.sum(earlier.astype(jnp.int32), axis=1, keepdims=True)
    chosen = rank == place
    order = jnp.sum(jnp.where(chosen, spot, 0), axis=0, keepdims=True)
    ordered = jnp.sum(jnp.where(chosen, target_of, 0), axis=0, keepdims=True)
    shifted = pltpu.roll(ordered, 1, 1)
    same = jnp.where((shifted == ordered) & (place[0:1] > 0), 1, 0)
    upto = jnp.sum((target_of <= place).astype(jnp.int32), axis=0, keepdims=True)
    here = jnp.sum((target_of == place).astype(jnp.int32), axis=0, keepdims=True)
    rank_rows[0:1] = order
    rank_rows[1:2] = same
    rank_rows[2:3] = jnp.maximum(upto - 1, 0)
    rank_rows[3:4] = jnp.where(here > 0, 1, 0)
    rank_rows[4:8] = jnp.zeros((4, rows), jnp.int32)
    load_table = pltpu.make_async_copy(rank_rows, table, table_sem)
    load_table.start()

    sources = (diag_hbm, next_hbm, prec_hbm)

    def stage_copy(chunk, which):
        slot = lax.rem(chunk, 2)
        return pltpu.make_async_copy(
            sources[which].at[pl.ds(chunk * CHUNK, CHUNK)],
            stage.at[slot, which],
            stage_sem.at[slot, which],
        )

    for which in range(3):
        stage_copy(0, which).start()
    trace[...] = jnp.zeros_like(trace)
    row = lax.broadcasted_iota(jnp.int32, (rows, rows), 0)
    col = lax.broadcasted_iota(jnp.int32, (rows, rows), 1)
    eye = row == col
    chunks = count // CHUNK

    @pl.loop(0, chunks)
    def _(chunk):
        @pl.when(chunk + 1 < chunks)
        def _():
            for which in range(3):
                stage_copy(chunk + 1, which).start()

        for which in range(3):
            stage_copy(chunk, which).wait()
        slot = lax.rem(chunk, 2)

        @pl.loop(0, CHUNK)
        def _(i):
            g = chunk * CHUNK + i
            here = stage[slot, 0, i]
            onto = stage[slot, 1, i]
            prec = stage[slot, 2, i]
            trace[...] += jnp.sum((here * prec).reshape(rows // 8, 8, rows), axis=0)
            diag_a[g] = jnp.sum(jnp.where(eye, here, 0.0), axis=0, keepdims=True)
            diag_p[g] = jnp.sum(jnp.where(eye, prec, 0.0), axis=0, keepdims=True)
            high, low = split(jnp.where(eye, 0.0, here))
            wa[g, 0:rows, 0:rows] = high
            wa[g, 0:rows, rows : 2 * rows] = low
            wrap = jnp.logical_and(g == count - 1, me == devices - 1)
            link = jnp.where(wrap, 0.0, links_ref[g].astype(F32))
            onto = onto * link
            high, low = split(onto)
            wa[g + 1, 2 * rows : 3 * rows, 0:rows] = high
            wa[g + 1, 2 * rows : 3 * rows, rows : 2 * rows] = low
            high, low = split(onto.T)
            wa[g, rows : 2 * rows, 0:rows] = high
            wa[g, rows : 2 * rows, rows : 2 * rows] = low
            high, low = split(jnp.where(eye, 0.0, prec))
            wp[g, :, 0:rows] = high
            wp[g, :, rows : 2 * rows] = low

    def reduce_over(phase, value):
        def dom_copy(peer, slot):
            return pltpu.make_async_remote_copy(
                src_ref=red_src.at[phase, 0],
                dst_ref=red_dom.at[phase, slot],
                send_sem=dom_send.at[phase, peer],
                recv_sem=dom_recv.at[phase, slot],
                device_id=(peer, me_sub),
                device_id_type=MESH,
            )

        def sub_copy(peer, slot):
            return pltpu.make_async_remote_copy(
                src_ref=red_src.at[phase, 1],
                dst_ref=red_sub.at[phase, slot],
                send_sem=sub_send.at[phase, peer],
                recv_sem=sub_recv.at[phase, slot],
                device_id=(me_dom, peer),
                device_id_type=MESH,
            )

        def begin():
            red_src[phase, 0] = value
            red_dom[phase, me_dom] = value

            @pl.loop(1, doms)
            def _(j):
                dom_copy((me_dom + j) & (doms - 1), me_dom).start()

        def middle_stage():
            @pl.loop(1, doms)
            def _(j):
                other = (me_dom + j) & (doms - 1)
                dom_copy(other, other).wait_recv()

            total = red_dom[phase, 0]
            for j in range(1, doms):
                total = total + red_dom[phase, j]
            red_src[phase, 1] = total
            red_sub[phase, me_sub] = total

            @pl.loop(1, subs)
            def _(j):
                sub_copy((me_sub + j) & (subs - 1), me_sub).start()

        def finish():
            @pl.loop(1, subs)
            def _(j):
                other = (me_sub + j) & (subs - 1)
                sub_copy(other, other).wait_recv()

            total = red_sub[phase, 0]
            for j in range(1, subs):
                total = total + red_sub[phase, j]

            @pl.loop(1, doms)
            def _(j):
                dom_copy((me_dom + j) & (doms - 1), me_dom).wait_send()

            @pl.loop(1, subs)
            def _(j):
                sub_copy((me_sub + j) & (subs - 1), me_sub).wait_send()

            return total

        return begin, middle_stage, finish

    link_copy = pltpu.make_async_remote_copy(
        src_ref=wa.at[count, pl.ds(2 * rows, rows)],
        dst_ref=wa.at[0, pl.ds(2 * rows, rows)],
        send_sem=link_send,
        recv_sem=link_recv,
        device_id=after_id,
        device_id_type=MESH,
    )
    link_copy.start()
    begin, middle_stage, finish = reduce_over(0, trace[...])
    begin()
    load_table.wait()

    others = pl.ds(0, devices - 1)
    load_mixed.wait()
    pltpu.make_async_copy(in_a.at[others], in_a.at[others], a_recv).wait()

    def code_tiles(peers):
        spots = [relay_ref[peer] for peer in peers]
        values_of = [
            jnp.dot(in_a[spot], mixed[spot], preferred_element_type=F32) for spot in spots
        ]
        tops = [jnp.max(jnp.abs(tile), axis=(0, 1), keepdims=True) for tile in values_of]
        units = [jnp.where(top > 0.0, top, 1.0) / LEVELS for top in tops]
        codes = [jnp.round(tile * (1.0 / unit)) for tile, unit in zip(values_of, units)]
        for peer, code, unit in zip(peers, codes, units):
            out_b[peer] = code.astype(jnp.int32).astype(jnp.int16)
            unit_out[peer] = jnp.broadcast_to(unit, (1, rows))

    def send_tile(peer):
        for source, target, send, receive in (
            (out_b, tiles, b_send, b_recv),
            (unit_out, unit_in, c_send, c_recv),
        ):
            pltpu.make_async_remote_copy(
                src_ref=source.at[peer],
                dst_ref=target.at[me],
                send_sem=send,
                recv_sem=receive,
                device_id=id_of(peer),
                device_id_type=MESH,
            ).start()

    def group_of(i):
        return tuple(peer_of(i * GROUP + 1 + j) for j in range(GROUP))

    first = group_of(0)
    code_tiles(first)

    def next_tiles(i, ready):
        peers = group_of(i)
        code_tiles(peers)
        for peer in ready:
            send_tile(peer)
        return peers

    ready = lax.fori_loop(1, devices // GROUP, next_tiles, first)
    tiles[me] = out_b[me]
    unit_in[me] = unit_out[me]
    for peer in ready[:-1]:
        send_tile(peer)
    middle_stage()
    pltpu.make_async_copy(out_a.at[others], out_a.at[others], a_send).wait()
    pltpu.make_async_copy(out_b.at[others], out_b.at[others], b_send).wait()
    pltpu.make_async_copy(tiles.at[others], tiles.at[others], b_recv).wait()
    pltpu.make_async_copy(unit_out.at[others], unit_out.at[others], c_send).wait()
    pltpu.make_async_copy(unit_in.at[others], unit_in.at[others], c_recv).wait()

    theta = finish()
    theta = jnp.sum(jnp.sum(theta, axis=0, keepdims=True), axis=1, keepdims=True)
    inv[...] = jnp.broadcast_to((1.0 * devices * count * rows) / theta, inv.shape)


    def add_tile(j, running):
        spot = jnp.clip(table[0, j], 0, slots - 1)
        tile = tiles[spot].astype(jnp.int32).astype(F32) * unit_in[spot]
        running = running * table[1, j].astype(F32) + tile
        red[j] = running
        return running

    lax.fori_loop(0, slots, add_tile, jnp.zeros((values, rows), F32))

    @pl.loop(0, count)
    def _(g):
        res[0, g] = red[jnp.clip(table[2, g], 0, slots - 1)] * table[3, g].astype(F32)

    def precondition(blocks, k, fields):
        outs = [
            product(stacked(field), wp[g], values) + field * diag_p[g]
            for g, field in zip(blocks, fields)
        ]
        for g, out in zip(blocks, outs):
            red[k * count + g] = out
            xs[k % 2, g + 1] = stacked(out)

    def apply_blocks(blocks, k, operands):
        fields = [red[k * count + g] for g in blocks]
        nows = [res[k, g] for g in blocks]
        befores = [res[k - 1, g] for g in blocks] if k > 0 else None
        images = [
            product(operand, wa[g], values) + field * diag_a[g]
            for g, field, operand in zip(blocks, fields, operands)
        ]
        laters = [now - image * inv[0:1] for now, image in zip(nows, images)]
        steps = [now - later for now, later in zip(nows, laters)]

        def dots(slot, left, right):
            acc[slot] += sum(a * b for a, b in zip(left, right))

        if k + 1 < STEPS:
            precondition(blocks, k + 1, laters)
        for g, later in zip(blocks, laters):
            res[k + 1, g] = later
        if k == 0:
            dots(0, fields, steps)
        else:
            dots(2 * k - 1, fields, [x - y for x, y in zip(befores, nows)])
            dots(2 * k, fields, steps)
        if k == 2:
            dots(5, [red[g] for g in blocks], laters)
            dots(6, [red[count + g] for g in blocks], laters)
            dots(7, fields, laters)

    def inner(g, k, width):
        near = [xs[k % 2, g + i] for i in range(width + 2)]
        apply_blocks(
            tuple(g + i for i in range(width)),
            k,
            [
                jnp.concatenate([near[i + 1], near[i + 2], near[i]], axis=1)
                for i in range(width)
            ],
        )

    def inners(start, stop, k):
        whole = (stop - start) // BATCH

        @pl.loop(0, whole)
        def _(i):
            inner(start + BATCH * i, k, BATCH)

        if (stop - start) % BATCH:
            inner(start + BATCH * whole, k, (stop - start) % BATCH)

    def preconditions(start, stop):
        whole = (stop - start) // BATCH

        def some(g, width):
            blocks = tuple(g + i for i in range(width))
            precondition(blocks, 0, [res[0, block] for block in blocks])

        @pl.loop(0, whole)
        def _(i):
            some(start + BATCH * i, BATCH)

        if (stop - start) % BATCH:
            some(start + BATCH * whole, (stop - start) % BATCH)

    def halo_copy(k, side):
        return pltpu.make_async_remote_copy(
            src_ref=xs.at[k % 2, count if side == 0 else 1],
            dst_ref=halo.at[k, side],
            send_sem=halo_send.at[k, side],
            recv_sem=halo_recv.at[k, side],
            device_id=after_id if side == 0 else before_id,
            device_id_type=MESH,
        )

    edges = (0, count - 1)
    middle = count // 2 + 1
    acc[...] = jnp.zeros_like(acc)
    precondition(edges, 0, [res[0, g] for g in edges])
    preconditions(1, 9)
    halo_copy(0, 0).start()
    halo_copy(0, 1).start()
    preconditions(9, count - 1)

    link_copy.wait()
    for k in range(STEPS):
        inners(1, middle, k)
        halo_copy(k, 0).wait()
        halo_copy(k, 1).wait()
        buf = k % 2
        apply_blocks(
            edges,
            k,
            [
                jnp.concatenate([xs[buf, 1], xs[buf, 2], halo[k, 0]], axis=1),
                jnp.concatenate([xs[buf, count], halo[k, 1], xs[buf, count - 1]], axis=1),
            ],
        )
        inners(middle, middle + 4, k)
        if k + 1 < STEPS:
            halo_copy(k + 1, 0).start()
            halo_copy(k + 1, 1).start()
        inners(middle + 4, count - 1, k)

    lane = lax.broadcasted_iota(jnp.int32, (values, rows), 1)
    packed = jnp.zeros((values, rows), F32)
    for j in range(8):
        packed = packed + jnp.where(lane == j, jnp.sum(acc[j], axis=1, keepdims=True), 0.0)
    packed = jnp.concatenate([packed, jnp.zeros((rows - values, rows), F32)], axis=0)
    begin, middle_stage, finish = reduce_over(1, packed.T[0:8])
    begin()
    middle_stage()
    total = finish()

    def over(top, bottom):
        usable = bottom != 0.0
        return jnp.where(usable, top / jnp.where(usable, bottom, 1.0), 0.0)

    g00, g10, g11, g21, g22 = (total[j : j + 1] for j in range(5))
    h0, h1, h2 = (-total[j : j + 1] for j in range(5, 8))
    l1, l2 = over(g10, g00), over(g11, g00)
    d1 = g11 - l1 * g10
    mix = g21 - l2 * g10
    l3 = over(mix, d1)
    d2 = g22 - l2 * g11 - l3 * mix
    y1 = h1 - l1 * h0
    y2 = h2 - l2 * h0 - l3 * y1
    e2 = over(y2, d2)
    e1 = over(y1, d1) - l3 * e2
    e0 = over(h0, g00) - l1 * e1 - l2 * e2
    weights = jnp.concatenate([e0, e1, e2, jnp.zeros((rows - 3, rows), F32)], axis=0).T
    e0 = jnp.broadcast_to(weights[0:values, 0:1], (values, rows))
    e1 = jnp.broadcast_to(weights[0:values, 1:2], (values, rows))
    e2 = jnp.broadcast_to(weights[0:values, 2:3], (values, rows))
    scale = inv[0:1]
    x0, x1, x2 = (1.0 - e0) * scale, (1.0 - e1) * scale, (1.0 - e2) * scale
    r1, r2, r3 = e1 - e0, e2 - e1, 1.0 - e2

    @pl.loop(0, count)
    def _(g):
        u0, u1, u2 = red[g], red[count + g], red[2 * count + g]
        red[g] = x0 * u0 + x1 * u1 + x2 * u2
        res[0, g] = e0 * res[0, g] + r1 * res[1, g] + r2 * res[2, g] + r3 * res[3, g]

    put_x = pltpu.make_async_copy(red.at[pl.ds(0, count)], x_hbm, out_sem.at[0])
    put_r = pltpu.make_async_copy(res.at[0], res_hbm, out_sem.at[1])
    put_x.start()
    put_r.start()
    put_x.wait()
    put_r.wait()


def mass_solve(target, links, pick, live, relay, history, mixed, mass_diag, mass_next, precond):
    doms, subs = lax.axis_size("dom"), lax.axis_size("sub")
    slots = mixed.shape[0]
    blocks, values, rows = history.shape
    count = mass_diag.shape[0]
    shape = (doms, subs, count, values, rows, slots)

    def kernel(*refs):
        solve_kernel(shape, *refs)

    smem = pl.BlockSpec(memory_space=pltpu.SMEM)
    hbm = pl.BlockSpec(memory_space=pl.ANY)
    field = jax.ShapeDtypeStruct((count, values, rows), F32)
    dma = pltpu.SemaphoreType.DMA
    return pl.pallas_call(
        kernel,
        out_shape=(field, field),
        in_specs=[pl.BlockSpec(memory_space=pltpu.VMEM)] + [smem] * 4 + [hbm] * 5,
        out_specs=(hbm, hbm),
        scratch_shapes=[
            pltpu.VMEM((blocks, values, rows), BF16),
            pltpu.VMEM((slots, rows, rows), BF16),
            pltpu.VMEM((slots, values, rows), BF16),
            pltpu.VMEM((slots, values, rows), BF16),
            pltpu.VMEM((slots, values, rows), jnp.int16),
            pltpu.VMEM((slots, values, rows), jnp.int16),
            pltpu.VMEM((slots, 1, rows), F32),
            pltpu.VMEM((slots, 1, rows), F32),
            pltpu.VMEM((2, 3, CHUNK, rows, rows), F32),
            pltpu.VMEM((count + 1, 3 * rows, 2 * rows), BF16),
            pltpu.VMEM((count, rows, 2 * rows), BF16),
            pltpu.VMEM((count, 1, rows), F32),
            pltpu.VMEM((count, 1, rows), F32),
            pltpu.VMEM((STEPS + 1, count, values, rows), F32),
            pltpu.VMEM((STEPS * count, values, rows), F32),
            pltpu.VMEM((2, count + 2, 2 * values, rows), BF16),
            pltpu.VMEM((STEPS, 2, 2 * values, rows), BF16),
            pltpu.VMEM((8, values, rows), F32),
            pltpu.VMEM((8, rows), F32),
            pltpu.VMEM((8, rows), F32),
            pltpu.VMEM((2, 2, 8, rows), F32),
            pltpu.VMEM((2, doms, 8, rows), F32),
            pltpu.VMEM((2, subs, 8, rows), F32),
            pltpu.VMEM((8, rows), jnp.int32),
            pltpu.SMEM((8, rows), jnp.int32),
            dma,
            pltpu.SemaphoreType.REGULAR((2,)),
            dma,
            dma,
            dma,
            dma,
            dma,
            dma,
            dma,
            dma,
            dma((2, 3)),
            dma((STEPS, 2)),
            dma((STEPS, 2)),
            dma,
            dma,
            dma((2, doms)),
            dma((2, doms)),
            dma((2, subs)),
            dma((2, subs)),
            dma((2,)),
        ],
        compiler_params=pltpu.CompilerParams(
            collective_id=0, has_side_effects=True, vmem_limit_bytes=60 * 1024 * 1024
        ),
    )(target, links, pick, live, relay, history, mixed, mass_diag, mass_next, precond)


def body(
    history,
    send_list,
    send_count,
    mixed_mass,
    relay_list,
    relay_target,
    mass_diag,
    mass_next,
    coupling,
    precond,
):
    return mass_solve(
        relay_target.reshape(1, -1),
        coupling,
        send_list.reshape(-1),
        send_count.reshape(-1),
        relay_list.reshape(-1),
        history,
        mixed_mass,
        mass_diag,
        mass_next,
        precond,
    )


def solution(mesh):
    whole = ("dom", "sub")
    placed = (
        P(whole, None, None),
        P(whole, None, None),
        P(whole, None),
        P(whole, None, None),
        P(whole, None, None),
        P(whole, None, None),
        P(whole, None, None),
        P(whole, None, None),
        P(whole),
        P(whole, None, None),
    )
    return jax.shard_map(
        body,
        mesh=mesh,
        in_specs=placed,
        out_specs=(P(whole, None, None), P(whole, None, None)),
        check_vma=False,
    )
```

```python
import jax
import jax.numpy as jnp
from jax import lax
from jax.experimental import pallas as pl
from jax.experimental.pallas import tpu as pltpu
from jax.sharding import PartitionSpec as P

MESH = pl.DeviceIdType.MESH
F32 = jnp.float32
BF16 = jnp.bfloat16
STEPS = 3
CHUNK = 4
ORDER = 37
GROUP = 4
PIECE = 8
LIMIT1 = 46000
LIMIT2 = 8000
BATCH = 8
LEVELS = 32767.0
FIRST_BITS = 0b0101010


def split(value):
    high = value.astype(BF16)
    low = (value - high.astype(F32)).astype(BF16)
    return high, low


def stacked(value):
    return jnp.concatenate(split(value), axis=0)


def product(left, weights, half):
    full = jnp.dot(left, weights, preferred_element_type=F32)
    top = full[:half] + full[half:]
    width = top.shape[1] // 2
    return top[:, :width] + top[:, width:]


def solve_kernel(
    shape,
    target_ref,
    links_ref,
    pick_ref,
    live_ref,
    relay_ref,
    hist_hbm,
    mixed_hbm,
    diag_hbm,
    next_hbm,
    prec_hbm,
    res,
    red,
    mix_ref,
    hist,
    mixed,
    out_a,
    in_a,
    out_b,
    tiles,
    unit_out,
    unit_in,
    stage,
    wa,
    wp,
    diag_a,
    diag_p,
    xs,
    halo,
    acc,
    trace,
    inv,
    red_src,
    red_dom,
    red_sub,
    rank_rows,
    table,
    table_sem,
    enter,
    hist_sem,
    mixed_sem,
    a_send,
    a_recv,
    b_send,
    b_recv,
    c_send,
    c_recv,
    stage_sem,
    halo_send,
    halo_recv,
    link_send,
    link_recv,
    dom_send,
    dom_recv,
    sub_send,
    sub_recv,
):
    doms, subs, count, values, rows, slots = shape
    devices = doms * subs
    me_dom, me_sub = lax.axis_index("dom"), lax.axis_index("sub")
    me = me_dom * subs + me_sub
    after = lax.rem(me + 1, devices)
    before = lax.rem(me + devices - 1, devices)
    after_id = (after // subs, lax.rem(after, subs))
    before_id = (before // subs, lax.rem(before, subs))

    load_hist = pltpu.make_async_copy(hist_hbm, hist, hist_sem)
    load_hist.start()
    load_mixed = pltpu.make_async_copy(mixed_hbm, mixed, mixed_sem)

    def peer_of(s):
        place = (s * ORDER) & (devices - 1)
        carry = (place & me & FIRST_BITS) << 1
        return place ^ me ^ carry

    def id_of(peer):
        return (peer >> 3, peer & (subs - 1))

    width = 4
    me_y, me_x = me_dom >> 2, me_dom & (width - 1)

    def line_x(j):
        return (me_y * width + ((me_x + j) & (width - 1)), me_sub)

    def line_y(j):
        return (((me_y + j) & (width - 1)) * width + me_x, me_sub)

    barrier = pltpu.get_barrier_semaphore()
    for j in range(1, subs):
        other = (me_dom, (me_sub + j) & (subs - 1))
        pl.semaphore_signal(barrier, inc=1, device_id=other, device_id_type=MESH)
    for j in range(1, width):
        pl.semaphore_signal(barrier, inc=1, device_id=line_x(j), device_id_type=MESH)
        pl.semaphore_signal(barrier, inc=1, device_id=line_y(j), device_id_type=MESH)

    pl.semaphore_wait(barrier, subs - 1 + 2 * (width - 1))
    for j in range(1, width):
        pl.semaphore_signal(enter.at[0], inc=1, device_id=line_x(j), device_id_type=MESH)
    pl.semaphore_wait(enter.at[0], width - 1)
    for j in range(1, width):
        pl.semaphore_signal(enter.at[1], inc=1, device_id=line_y(j), device_id_type=MESH)

    load_hist.wait()

    @pl.loop(0, devices)
    def _(e):
        block = hist[pick_ref[e]]
        out_a[e] = jnp.where(live_ref[e] > 0, block, jnp.zeros_like(block))

    pl.semaphore_wait(enter.at[1], width - 1)

    @pl.loop(1, devices)
    def _(s):
        peer = peer_of(s)
        pltpu.make_async_remote_copy(
            src_ref=out_a.at[peer],
            dst_ref=in_a.at[me],
            send_sem=a_send,
            recv_sem=a_recv,
            device_id=id_of(peer),
            device_id_type=MESH,
        ).start()

    in_a[me] = out_a[me]
    load_mixed.start()

    spot = lax.broadcasted_iota(jnp.int32, (slots, slots), 0)
    place = lax.broadcasted_iota(jnp.int32, (slots, slots), 1)
    target = jnp.broadcast_to(target_ref[...], (slots, slots))
    target_of = jnp.sum(jnp.where(spot == place, target, 0), axis=1, keepdims=True)
    earlier = target * slots + place < target_of * slots + spot
    rank = jnp.sum(earlier.astype(jnp.int32), axis=1, keepdims=True)
    chosen = rank == place
    order = jnp.sum(jnp.where(chosen, spot, 0), axis=0, keepdims=True)
    ordered = jnp.sum(jnp.where(chosen, target_of, 0), axis=0, keepdims=True)
    shifted = pltpu.roll(ordered, 1, 1)
    same = jnp.where((shifted == ordered) & (place[0:1] > 0), 1, 0)
    upto = jnp.sum((target_of <= place).astype(jnp.int32), axis=0, keepdims=True)
    here = jnp.sum((target_of == place).astype(jnp.int32), axis=0, keepdims=True)
    rank_rows[0:1] = order
    rank_rows[1:2] = same
    rank_rows[2:3] = jnp.maximum(upto - 1, 0)
    rank_rows[3:4] = jnp.where(here > 0, 1, 0)
    rank_rows[4:8] = jnp.zeros((4, rows), jnp.int32)
    load_table = pltpu.make_async_copy(rank_rows, table, table_sem)
    load_table.start()

    sources = (diag_hbm, next_hbm, prec_hbm)

    def stage_copy(chunk, which):
        slot = lax.rem(chunk, 2)
        return pltpu.make_async_copy(
            sources[which].at[pl.ds(chunk * CHUNK, CHUNK)],
            stage.at[slot, which],
            stage_sem.at[slot, which],
        )

    for which in range(3):
        stage_copy(0, which).start()
    trace[...] = jnp.zeros_like(trace)
    row = lax.broadcasted_iota(jnp.int32, (rows, rows), 0)
    col = lax.broadcasted_iota(jnp.int32, (rows, rows), 1)
    eye = row == col
    chunks = count // CHUNK

    @pl.loop(0, chunks)
    def _(chunk):
        @pl.when(chunk + 1 < chunks)
        def _():
            for which in range(3):
                stage_copy(chunk + 1, which).start()

        for which in range(3):
            stage_copy(chunk, which).wait()
        slot = lax.rem(chunk, 2)

        @pl.loop(0, CHUNK)
        def _(i):
            g = chunk * CHUNK + i
            here = stage[slot, 0, i]
            onto = stage[slot, 1, i]
            prec = stage[slot, 2, i]
            trace[...] += jnp.sum((here * prec).reshape(rows // 8, 8, rows), axis=0)
            diag_a[g] = jnp.sum(jnp.where(eye, here, 0.0), axis=0, keepdims=True)
            diag_p[g] = jnp.sum(jnp.where(eye, prec, 0.0), axis=0, keepdims=True)
            high, low = split(jnp.where(eye, 0.0, here))
            wa[g, 0:rows, 0:rows] = high
            wa[g, 0:rows, rows : 2 * rows] = low
            wrap = jnp.logical_and(g == count - 1, me == devices - 1)
            link = jnp.where(wrap, 0.0, links_ref[g].astype(F32))
            onto = onto * link
            high, low = split(onto)
            wa[g + 1, 2 * rows : 3 * rows, 0:rows] = high
            wa[g + 1, 2 * rows : 3 * rows, rows : 2 * rows] = low
            high, low = split(onto.T)
            wa[g, rows : 2 * rows, 0:rows] = high
            wa[g, rows : 2 * rows, rows : 2 * rows] = low
            high, low = split(jnp.where(eye, 0.0, prec))
            wp[g, :, 0:rows] = high
            wp[g, :, rows : 2 * rows] = low

    def reduce_over(phase, value):
        def dom_copy(peer, slot):
            return pltpu.make_async_remote_copy(
                src_ref=red_src.at[phase, 0],
                dst_ref=red_dom.at[phase, slot],
                send_sem=dom_send.at[phase, peer],
                recv_sem=dom_recv.at[phase, slot],
                device_id=(peer, me_sub),
                device_id_type=MESH,
            )

        def sub_copy(peer, slot):
            return pltpu.make_async_remote_copy(
                src_ref=red_src.at[phase, 1],
                dst_ref=red_sub.at[phase, slot],
                send_sem=sub_send.at[phase, peer],
                recv_sem=sub_recv.at[phase, slot],
                device_id=(me_dom, peer),
                device_id_type=MESH,
            )

        def begin():
            red_src[phase, 0] = value
            red_dom[phase, me_dom] = value

            @pl.loop(1, doms)
            def _(j):
                dom_copy((me_dom + j) & (doms - 1), me_dom).start()

        def middle_stage():
            @pl.loop(1, doms)
            def _(j):
                other = (me_dom + j) & (doms - 1)
                dom_copy(other, other).wait_recv()

            total = red_dom[phase, 0]
            for j in range(1, doms):
                total = total + red_dom[phase, j]
            red_src[phase, 1] = total
            red_sub[phase, me_sub] = total

            @pl.loop(1, subs)
            def _(j):
                sub_copy((me_sub + j) & (subs - 1), me_sub).start()

        def finish():
            @pl.loop(1, subs)
            def _(j):
                other = (me_sub + j) & (subs - 1)
                sub_copy(other, other).wait_recv()

            total = red_sub[phase, 0]
            for j in range(1, subs):
                total = total + red_sub[phase, j]

            @pl.loop(1, doms)
            def _(j):
                dom_copy((me_dom + j) & (doms - 1), me_dom).wait_send()

            @pl.loop(1, subs)
            def _(j):
                sub_copy((me_sub + j) & (subs - 1), me_sub).wait_send()

            return total

        return begin, middle_stage, finish

    link_copy = pltpu.make_async_remote_copy(
        src_ref=wa.at[count, pl.ds(2 * rows, rows)],
        dst_ref=wa.at[0, pl.ds(2 * rows, rows)],
        send_sem=link_send,
        recv_sem=link_recv,
        device_id=after_id,
        device_id_type=MESH,
    )
    link_copy.start()
    begin, middle_stage, finish = reduce_over(0, trace[...])
    begin()
    load_table.wait()

    others = pl.ds(0, devices - 1)
    load_mixed.wait()
    pltpu.make_async_copy(in_a.at[others], in_a.at[others], a_recv).wait()

    def code_tiles(peers):
        spots = [relay_ref[peer] for peer in peers]
        values_of = [
            jnp.dot(in_a[spot], mixed[spot], preferred_element_type=F32) for spot in spots
        ]
        tops = [jnp.max(jnp.abs(tile), axis=(0, 1), keepdims=True) for tile in values_of]
        units = [jnp.where(top > 0.0, top, 1.0) / LEVELS for top in tops]
        codes = [jnp.round(tile * (1.0 / unit)) for tile, unit in zip(values_of, units)]
        for peer, code, unit in zip(peers, codes, units):
            out_b[peer] = code.astype(jnp.int32).astype(jnp.int16)
            unit_out[peer] = jnp.broadcast_to(unit, (1, rows))

    def send_tile(peer):
        for source, target, send, receive in (
            (out_b, tiles, b_send, b_recv),
            (unit_out, unit_in, c_send, c_recv),
        ):
            pltpu.make_async_remote_copy(
                src_ref=source.at[peer],
                dst_ref=target.at[me],
                send_sem=send,
                recv_sem=receive,
                device_id=id_of(peer),
                device_id_type=MESH,
            ).start()

    def group_of(i):
        return tuple(peer_of(i * GROUP + 1 + j) for j in range(GROUP))

    first = group_of(0)
    code_tiles(first)

    def next_tiles(i, ready):
        peers = group_of(i)
        code_tiles(peers)
        for peer in ready:
            send_tile(peer)
        return peers

    ready = lax.fori_loop(1, devices // GROUP, next_tiles, first)
    tiles[me] = out_b[me]
    unit_in[me] = unit_out[me]
    for peer in ready[:-1]:
        send_tile(peer)
    middle_stage()
    pltpu.make_async_copy(out_a.at[others], out_a.at[others], a_send).wait()
    pltpu.make_async_copy(out_b.at[others], out_b.at[others], b_send).wait()
    pltpu.make_async_copy(tiles.at[others], tiles.at[others], b_recv).wait()
    pltpu.make_async_copy(unit_out.at[others], unit_out.at[others], c_send).wait()
    pltpu.make_async_copy(unit_in.at[others], unit_in.at[others], c_recv).wait()

    theta = finish()
    theta = jnp.sum(jnp.sum(theta, axis=0, keepdims=True), axis=1, keepdims=True)
    inv[...] = jnp.broadcast_to((1.0 * devices * count * rows) / theta, inv.shape)


    def add_tile(j, running):
        spot = jnp.clip(table[0, j], 0, slots - 1)
        tile = tiles[spot].astype(jnp.int32).astype(F32) * unit_in[spot]
        running = running * table[1, j].astype(F32) + tile
        red[j] = running
        return running

    lax.fori_loop(0, slots, add_tile, jnp.zeros((values, rows), F32))

    @pl.loop(0, count)
    def _(g):
        res[0, g] = red[jnp.clip(table[2, g], 0, slots - 1)] * table[3, g].astype(F32)

    def precondition(blocks, k, fields):
        outs = [
            product(stacked(field), wp[g], values) + field * diag_p[g]
            for g, field in zip(blocks, fields)
        ]
        for g, out in zip(blocks, outs):
            red[k * count + g] = out
            xs[k % 2, g + 1] = stacked(out)

    def apply_blocks(blocks, k, operands):
        fields = [red[k * count + g] for g in blocks]
        nows = [res[k, g] for g in blocks]
        befores = [res[k - 1, g] for g in blocks] if k > 0 else None
        images = [
            product(operand, wa[g], values) + field * diag_a[g]
            for g, field, operand in zip(blocks, fields, operands)
        ]
        laters = [now - image * inv[0:1] for now, image in zip(nows, images)]
        steps = [now - later for now, later in zip(nows, laters)]

        def dots(slot, left, right):
            acc[slot] += sum(a * b for a, b in zip(left, right))

        if k + 1 < STEPS:
            precondition(blocks, k + 1, laters)
        for g, later in zip(blocks, laters):
            res[k + 1, g] = later
        if k == 0:
            dots(0, fields, steps)
        else:
            dots(2 * k - 1, fields, [x - y for x, y in zip(befores, nows)])
            dots(2 * k, fields, steps)
        if k == 2:
            dots(5, [red[g] for g in blocks], laters)
            dots(6, [red[count + g] for g in blocks], laters)
            dots(7, fields, laters)

    def inner(g, k, width):
        near = [xs[k % 2, g + i] for i in range(width + 2)]
        apply_blocks(
            tuple(g + i for i in range(width)),
            k,
            [
                jnp.concatenate([near[i + 1], near[i + 2], near[i]], axis=1)
                for i in range(width)
            ],
        )

    def inners(start, stop, k):
        whole = (stop - start) // BATCH

        @pl.loop(0, whole)
        def _(i):
            inner(start + BATCH * i, k, BATCH)

        if (stop - start) % BATCH:
            inner(start + BATCH * whole, k, (stop - start) % BATCH)

    def preconditions(start, stop):
        whole = (stop - start) // BATCH

        def some(g, width):
            blocks = tuple(g + i for i in range(width))
            precondition(blocks, 0, [res[0, block] for block in blocks])

        @pl.loop(0, whole)
        def _(i):
            some(start + BATCH * i, BATCH)

        if (stop - start) % BATCH:
            some(start + BATCH * whole, (stop - start) % BATCH)

    def halo_copy(k, side):
        return pltpu.make_async_remote_copy(
            src_ref=xs.at[k % 2, count if side == 0 else 1],
            dst_ref=halo.at[k, side],
            send_sem=halo_send.at[k, side],
            recv_sem=halo_recv.at[k, side],
            device_id=after_id if side == 0 else before_id,
            device_id_type=MESH,
        )

    edges = (0, count - 1)
    middle = count // 2 + 1
    acc[...] = jnp.zeros_like(acc)
    precondition(edges, 0, [res[0, g] for g in edges])
    preconditions(1, 9)
    halo_copy(0, 0).start()
    halo_copy(0, 1).start()
    preconditions(9, count - 1)

    link_copy.wait()
    for k in range(STEPS):
        inners(1, middle, k)
        halo_copy(k, 0).wait()
        halo_copy(k, 1).wait()
        buf = k % 2
        apply_blocks(
            edges,
            k,
            [
                jnp.concatenate([xs[buf, 1], xs[buf, 2], halo[k, 0]], axis=1),
                jnp.concatenate([xs[buf, count], halo[k, 1], xs[buf, count - 1]], axis=1),
            ],
        )
        inners(middle, middle + 4, k)
        if k + 1 < STEPS:
            halo_copy(k + 1, 0).start()
            halo_copy(k + 1, 1).start()
        inners(middle + 4, count - 1, k)

    lane = lax.broadcasted_iota(jnp.int32, (values, rows), 1)
    packed = jnp.zeros((values, rows), F32)
    for j in range(8):
        packed = packed + jnp.where(lane == j, jnp.sum(acc[j], axis=1, keepdims=True), 0.0)
    packed = jnp.concatenate([packed, jnp.zeros((rows - values, rows), F32)], axis=0)
    begin, middle_stage, finish = reduce_over(1, packed.T[0:8])
    begin()
    middle_stage()
    total = finish()

    def over(top, bottom):
        usable = bottom != 0.0
        return jnp.where(usable, top / jnp.where(usable, bottom, 1.0), 0.0)

    g00, g10, g11, g21, g22 = (total[j : j + 1] for j in range(5))
    h0, h1, h2 = (-total[j : j + 1] for j in range(5, 8))
    l1, l2 = over(g10, g00), over(g11, g00)
    d1 = g11 - l1 * g10
    mix = g21 - l2 * g10
    l3 = over(mix, d1)
    d2 = g22 - l2 * g11 - l3 * mix
    y1 = h1 - l1 * h0
    y2 = h2 - l2 * h0 - l3 * y1
    e2 = over(y2, d2)
    e1 = over(y1, d1) - l3 * e2
    e0 = over(h0, g00) - l1 * e1 - l2 * e2
    weights = jnp.concatenate([e0, e1, e2, jnp.zeros((rows - 3, rows), F32)], axis=0).T
    e0 = jnp.broadcast_to(weights[0:values, 0:1], (values, rows))
    e1 = jnp.broadcast_to(weights[0:values, 1:2], (values, rows))
    e2 = jnp.broadcast_to(weights[0:values, 2:3], (values, rows))
    scale = inv[0:1]
    for j, factor in enumerate(
        ((1.0 - e0) * scale, (1.0 - e1) * scale, (1.0 - e2) * scale, e0, e1 - e0, e2 - e1, 1.0 - e2)
    ):
        mix_ref[j] = factor


def combine_kernel(res, red, mix_ref, x_hbm, res_hbm, x_all, r_all, sems):
    count, values, rows = x_all.shape
    x0, x1, x2, r0, r1, r2, r3 = (mix_ref[j] for j in range(7))
    pieces = count // PIECE

    def puts(piece):
        part = pl.ds(piece * PIECE, PIECE)
        return (
            pltpu.make_async_copy(x_all.at[part], x_hbm.at[part], sems.at[0, piece]),
            pltpu.make_async_copy(r_all.at[part], res_hbm.at[part], sems.at[1, piece]),
        )

    @pl.loop(0, pieces)
    def _(piece):
        @pl.loop(0, PIECE // 2)
        def _(i):
            for j in range(2):
                g = piece * PIECE + 2 * i + j
                x_all[g] = x0 * red[g] + x1 * red[count + g] + x2 * red[2 * count + g]
                r_all[g] = r0 * res[0, g] + r1 * res[1, g] + r2 * res[2, g] + r3 * res[3, g]

        for put in puts(piece):
            put.start()

    @pl.loop(0, pieces)
    def _(piece):
        for put in puts(piece):
            put.wait()


def mass_solve(target, links, pick, live, relay, history, mixed, mass_diag, mass_next, precond):
    doms, subs = lax.axis_size("dom"), lax.axis_size("sub")
    slots = mixed.shape[0]
    blocks, values, rows = history.shape
    count = mass_diag.shape[0]
    shape = (doms, subs, count, values, rows, slots)

    def kernel(*refs):
        solve_kernel(shape, *refs)

    smem = pl.BlockSpec(memory_space=pltpu.SMEM)
    hbm = pl.BlockSpec(memory_space=pl.ANY)
    field = jax.ShapeDtypeStruct((count, values, rows), F32)
    dma = pltpu.SemaphoreType.DMA
    vmem = pl.BlockSpec(memory_space=pltpu.VMEM)
    parts = (
        pltpu.VMEM((STEPS + 1, count, values, rows), F32),
        pltpu.VMEM((STEPS * count, values, rows), F32),
        pltpu.VMEM((7, values, rows), F32),
    )
    parts = pl.pallas_call(
        kernel,
        out_shape=parts,
        in_specs=[pl.BlockSpec(memory_space=pltpu.VMEM)] + [smem] * 4 + [hbm] * 5,
        out_specs=(vmem,) * 3,
        scratch_shapes=[
            pltpu.VMEM((blocks, values, rows), BF16),
            pltpu.VMEM((slots, rows, rows), BF16),
            pltpu.VMEM((slots, values, rows), BF16),
            pltpu.VMEM((slots, values, rows), BF16),
            pltpu.VMEM((slots, values, rows), jnp.int16),
            pltpu.VMEM((slots, values, rows), jnp.int16),
            pltpu.VMEM((slots, 1, rows), F32),
            pltpu.VMEM((slots, 1, rows), F32),
            pltpu.VMEM((2, 3, CHUNK, rows, rows), F32),
            pltpu.VMEM((count + 1, 3 * rows, 2 * rows), BF16),
            pltpu.VMEM((count, rows, 2 * rows), BF16),
            pltpu.VMEM((count, 1, rows), F32),
            pltpu.VMEM((count, 1, rows), F32),
            pltpu.VMEM((2, count + 2, 2 * values, rows), BF16),
            pltpu.VMEM((STEPS, 2, 2 * values, rows), BF16),
            pltpu.VMEM((8, values, rows), F32),
            pltpu.VMEM((8, rows), F32),
            pltpu.VMEM((8, rows), F32),
            pltpu.VMEM((2, 2, 8, rows), F32),
            pltpu.VMEM((2, doms, 8, rows), F32),
            pltpu.VMEM((2, subs, 8, rows), F32),
            pltpu.VMEM((8, rows), jnp.int32),
            pltpu.SMEM((8, rows), jnp.int32),
            dma,
            pltpu.SemaphoreType.REGULAR((2,)),
            dma,
            dma,
            dma,
            dma,
            dma,
            dma,
            dma,
            dma,
            dma((2, 3)),
            dma((STEPS, 2)),
            dma((STEPS, 2)),
            dma,
            dma,
            dma((2, doms)),
            dma((2, doms)),
            dma((2, subs)),
            dma((2, subs)),
        ],
        compiler_params=pltpu.CompilerParams(
            collective_id=0, has_side_effects=True, vmem_limit_bytes=LIMIT1 * 1024
        ),
    )(target, links, pick, live, relay, history, mixed, mass_diag, mass_next, precond)
    return pl.pallas_call(
        combine_kernel,
        out_shape=(field, field),
        in_specs=[vmem] * 3,
        out_specs=(hbm, hbm),
        scratch_shapes=[
            pltpu.VMEM((count, values, rows), F32),
            pltpu.VMEM((count, values, rows), F32),
            dma((2, count // PIECE)),
        ],
        compiler_params=pltpu.CompilerParams(vmem_limit_bytes=LIMIT2 * 1024),
    )(*parts)


def body(
    history,
    send_list,
    send_count,
    mixed_mass,
    relay_list,
    relay_target,
    mass_diag,
    mass_next,
    coupling,
    precond,
):
    return mass_solve(
        relay_target.reshape(1, -1),
        coupling,
        send_list.reshape(-1),
        send_count.reshape(-1),
        relay_list.reshape(-1),
        history,
        mixed_mass,
        mass_diag,
        mass_next,
        precond,
    )


def solution(mesh):
    whole = ("dom", "sub")
    placed = (
        P(whole, None, None),
        P(whole, None, None),
        P(whole, None),
        P(whole, None, None),
        P(whole, None, None),
        P(whole, None, None),
        P(whole, None, None),
        P(whole, None, None),
        P(whole),
        P(whole, None, None),
    )
    return jax.shard_map(
        body,
        mesh=mesh,
        in_specs=placed,
        out_specs=(P(whole, None, None), P(whole, None, None)),
        check_vma=False,
    )
```

```python
import jax
import jax.numpy as jnp
from jax import lax
from jax.experimental import pallas as pl
from jax.experimental.pallas import tpu as pltpu
from jax.sharding import PartitionSpec as P

MESH = pl.DeviceIdType.MESH
F32 = jnp.float32
BF16 = jnp.bfloat16
STEPS = 3
CHUNK = 4
ORDER = 37
GROUP = 4
PARTS = 2
SMALLEST = 1e-30
PIECE = 8
LIMIT1 = 46000
LIMIT2 = 8000
BATCH = 8
LEVELS = 32767.0
FIRST_BITS = 0b0101010


def split(value):
    high = value.astype(BF16)
    low = (value - high.astype(F32)).astype(BF16)
    return high, low


def stacked(value):
    return jnp.concatenate(split(value), axis=0)


def product(left, weights, half):
    full = jnp.dot(left, weights, preferred_element_type=F32)
    top = full[:half] + full[half:]
    width = top.shape[1] // 2
    return top[:, :width] + top[:, width:]


def solve_kernel(
    shape,
    target_ref,
    links_ref,
    pick_ref,
    live_ref,
    relay_ref,
    hist_hbm,
    mixed_hbm,
    diag_hbm,
    next_hbm,
    prec_hbm,
    res,
    red,
    mix_ref,
    hist,
    mixed,
    out_a,
    in_a_0,
    in_a_1,
    out_b,
    tiles_0,
    tiles_1,
    unit_out,
    unit_in_0,
    unit_in_1,
    stage,
    wa,
    wp,
    diag_a,
    diag_p,
    xs,
    halo,
    acc,
    trace,
    inv,
    red_src,
    red_dom,
    red_sub,
    rank_rows,
    table,
    table_sem,
    enter,
    hist_sem,
    mixed_sem,
    a_send,
    a_recv,
    b_send,
    b_recv,
    c_send,
    c_recv,
    stage_sem,
    halo_send,
    halo_recv,
    link_send,
    link_recv,
    dom_send,
    dom_recv,
    sub_send,
    sub_recv,
):
    doms, subs, count, values, rows, slots = shape
    devices = doms * subs
    part = values // PARTS
    in_a, tiles, unit_in = (in_a_0, in_a_1), (tiles_0, tiles_1), (unit_in_0, unit_in_1)
    me_dom, me_sub = lax.axis_index("dom"), lax.axis_index("sub")
    me = me_dom * subs + me_sub
    after = lax.rem(me + 1, devices)
    before = lax.rem(me + devices - 1, devices)
    after_id = (after // subs, lax.rem(after, subs))
    before_id = (before // subs, lax.rem(before, subs))

    load_hist = pltpu.make_async_copy(hist_hbm, hist, hist_sem)
    load_hist.start()
    load_mixed = pltpu.make_async_copy(mixed_hbm, mixed, mixed_sem)

    def peer_of(s):
        place = (s * ORDER) & (devices - 1)
        carry = (place & me & FIRST_BITS) << 1
        return place ^ me ^ carry

    def id_of(peer):
        return (peer >> 3, peer & (subs - 1))

    width = 4
    me_y, me_x = me_dom >> 2, me_dom & (width - 1)

    def line_x(j):
        return (me_y * width + ((me_x + j) & (width - 1)), me_sub)

    def line_y(j):
        return (((me_y + j) & (width - 1)) * width + me_x, me_sub)

    barrier = pltpu.get_barrier_semaphore()
    for j in range(1, subs):
        other = (me_dom, (me_sub + j) & (subs - 1))
        pl.semaphore_signal(barrier, inc=1, device_id=other, device_id_type=MESH)
    for j in range(1, width):
        pl.semaphore_signal(barrier, inc=1, device_id=line_x(j), device_id_type=MESH)
        pl.semaphore_signal(barrier, inc=1, device_id=line_y(j), device_id_type=MESH)

    pl.semaphore_wait(barrier, subs - 1 + 2 * (width - 1))
    for j in range(1, width):
        pl.semaphore_signal(enter.at[0], inc=1, device_id=line_x(j), device_id_type=MESH)
    pl.semaphore_wait(enter.at[0], width - 1)
    for j in range(1, width):
        pl.semaphore_signal(enter.at[1], inc=1, device_id=line_y(j), device_id_type=MESH)

    load_hist.wait()

    @pl.loop(0, devices)
    def _(e):
        block = hist[pick_ref[e]]
        block = jnp.where(live_ref[e] > 0, block, jnp.zeros_like(block))
        for h in range(PARTS):
            out_a[h, e] = block[h * part : (h + 1) * part]

    pl.semaphore_wait(enter.at[1], width - 1)

    for h in range(PARTS):

        @pl.loop(1, devices)
        def _(s):
            peer = peer_of(s)
            pltpu.make_async_remote_copy(
                src_ref=out_a.at[h, peer],
                dst_ref=in_a[h].at[me],
                send_sem=a_send.at[h],
                recv_sem=a_recv.at[h],
                device_id=id_of(peer),
                device_id_type=MESH,
            ).start()

    for h in range(PARTS):
        in_a[h][me] = out_a[h, me]
    load_mixed.start()

    spot = lax.broadcasted_iota(jnp.int32, (slots, slots), 0)
    place = lax.broadcasted_iota(jnp.int32, (slots, slots), 1)
    target = jnp.broadcast_to(target_ref[...], (slots, slots))
    target_of = jnp.sum(jnp.where(spot == place, target, 0), axis=1, keepdims=True)
    earlier = target * slots + place < target_of * slots + spot
    rank = jnp.sum(earlier.astype(jnp.int32), axis=1, keepdims=True)
    chosen = rank == place
    order = jnp.sum(jnp.where(chosen, spot, 0), axis=0, keepdims=True)
    ordered = jnp.sum(jnp.where(chosen, target_of, 0), axis=0, keepdims=True)
    shifted = pltpu.roll(ordered, 1, 1)
    same = jnp.where((shifted == ordered) & (place[0:1] > 0), 1, 0)
    upto = jnp.sum((target_of <= place).astype(jnp.int32), axis=0, keepdims=True)
    here = jnp.sum((target_of == place).astype(jnp.int32), axis=0, keepdims=True)
    rank_rows[0:1] = order
    rank_rows[1:2] = same
    rank_rows[2:3] = jnp.maximum(upto - 1, 0)
    rank_rows[3:4] = jnp.where(here > 0, 1, 0)
    rank_rows[4:8] = jnp.zeros((4, rows), jnp.int32)
    load_table = pltpu.make_async_copy(rank_rows, table, table_sem)
    load_table.start()

    sources = (diag_hbm, next_hbm, prec_hbm)

    def stage_copy(chunk, which):
        slot = lax.rem(chunk, 2)
        return pltpu.make_async_copy(
            sources[which].at[pl.ds(chunk * CHUNK, CHUNK)],
            stage.at[slot, which],
            stage_sem.at[slot, which],
        )

    for which in range(3):
        stage_copy(0, which).start()
    trace[...] = jnp.zeros_like(trace)
    row = lax.broadcasted_iota(jnp.int32, (rows, rows), 0)
    col = lax.broadcasted_iota(jnp.int32, (rows, rows), 1)
    eye = row == col
    chunks = count // CHUNK

    @pl.loop(0, chunks)
    def _(chunk):
        @pl.when(chunk + 1 < chunks)
        def _():
            for which in range(3):
                stage_copy(chunk + 1, which).start()

        for which in range(3):
            stage_copy(chunk, which).wait()
        slot = lax.rem(chunk, 2)

        @pl.loop(0, CHUNK)
        def _(i):
            g = chunk * CHUNK + i
            here = stage[slot, 0, i]
            onto = stage[slot, 1, i]
            prec = stage[slot, 2, i]
            trace[...] += jnp.sum((here * prec).reshape(rows // 8, 8, rows), axis=0)
            diag_a[g] = jnp.sum(jnp.where(eye, here, 0.0), axis=0, keepdims=True)
            diag_p[g] = jnp.sum(jnp.where(eye, prec, 0.0), axis=0, keepdims=True)
            high, low = split(jnp.where(eye, 0.0, here))
            wa[g, 0:rows, 0:rows] = high
            wa[g, 0:rows, rows : 2 * rows] = low
            wrap = jnp.logical_and(g == count - 1, me == devices - 1)
            link = jnp.where(wrap, 0.0, links_ref[g].astype(F32))
            onto = onto * link
            high, low = split(onto)
            wa[g + 1, 2 * rows : 3 * rows, 0:rows] = high
            wa[g + 1, 2 * rows : 3 * rows, rows : 2 * rows] = low
            high, low = split(onto.T)
            wa[g, rows : 2 * rows, 0:rows] = high
            wa[g, rows : 2 * rows, rows : 2 * rows] = low
            high, low = split(jnp.where(eye, 0.0, prec))
            wp[g, :, 0:rows] = high
            wp[g, :, rows : 2 * rows] = low

    def reduce_over(phase, value):
        def dom_copy(peer, slot):
            return pltpu.make_async_remote_copy(
                src_ref=red_src.at[phase, 0],
                dst_ref=red_dom.at[phase, slot],
                send_sem=dom_send.at[phase, peer],
                recv_sem=dom_recv.at[phase, slot],
                device_id=(peer, me_sub),
                device_id_type=MESH,
            )

        def sub_copy(peer, slot):
            return pltpu.make_async_remote_copy(
                src_ref=red_src.at[phase, 1],
                dst_ref=red_sub.at[phase, slot],
                send_sem=sub_send.at[phase, peer],
                recv_sem=sub_recv.at[phase, slot],
                device_id=(me_dom, peer),
                device_id_type=MESH,
            )

        def begin():
            red_src[phase, 0] = value
            red_dom[phase, me_dom] = value

            @pl.loop(1, doms)
            def _(j):
                dom_copy((me_dom + j) & (doms - 1), me_dom).start()

        def middle_stage():
            @pl.loop(1, doms)
            def _(j):
                other = (me_dom + j) & (doms - 1)
                dom_copy(other, other).wait_recv()

            total = red_dom[phase, 0]
            for j in range(1, doms):
                total = total + red_dom[phase, j]
            red_src[phase, 1] = total
            red_sub[phase, me_sub] = total

            @pl.loop(1, subs)
            def _(j):
                sub_copy((me_sub + j) & (subs - 1), me_sub).start()

        def finish():
            @pl.loop(1, subs)
            def _(j):
                other = (me_sub + j) & (subs - 1)
                sub_copy(other, other).wait_recv()

            total = red_sub[phase, 0]
            for j in range(1, subs):
                total = total + red_sub[phase, j]

            @pl.loop(1, doms)
            def _(j):
                dom_copy((me_dom + j) & (doms - 1), me_dom).wait_send()

            @pl.loop(1, subs)
            def _(j):
                sub_copy((me_sub + j) & (subs - 1), me_sub).wait_send()

            return total

        return begin, middle_stage, finish

    link_copy = pltpu.make_async_remote_copy(
        src_ref=wa.at[count, pl.ds(2 * rows, rows)],
        dst_ref=wa.at[0, pl.ds(2 * rows, rows)],
        send_sem=link_send,
        recv_sem=link_recv,
        device_id=after_id,
        device_id_type=MESH,
    )
    link_copy.start()
    begin, middle_stage, finish = reduce_over(0, trace[...])
    begin()
    load_table.wait()

    others = pl.ds(0, devices - 1)
    load_mixed.wait()

    def wait_all(buffer, h, semaphore):
        view = buffer.at[others]
        pltpu.make_async_copy(view, view, semaphore.at[h]).wait()

    def code_tiles(h, peers):
        spots = [relay_ref[peer] for peer in peers]
        values_of = [
            jnp.dot(in_a[h][spot], mixed[spot], preferred_element_type=F32) for spot in spots
        ]
        tops = [jnp.max(jnp.abs(tile), axis=(0, 1), keepdims=True) for tile in values_of]
        units = [jnp.maximum(top, SMALLEST) / LEVELS for top in tops]
        codes = [jnp.round(tile * (1.0 / unit)) for tile, unit in zip(values_of, units)]
        for peer, code, unit in zip(peers, codes, units):
            out_b[h, peer] = code.astype(jnp.int32).astype(jnp.int16)
            unit_out[h, peer] = jnp.broadcast_to(unit, (1, rows))

    def send_tile(h, peer):
        for source, target, send, receive in (
            (out_b, tiles, b_send, b_recv),
            (unit_out, unit_in, c_send, c_recv),
        ):
            pltpu.make_async_remote_copy(
                src_ref=source.at[h, peer],
                dst_ref=target[h].at[me],
                send_sem=send.at[h],
                recv_sem=receive.at[h],
                device_id=id_of(peer),
                device_id_type=MESH,
            ).start()

    def group_of(i):
        return tuple(peer_of(i * GROUP + 1 + j) for j in range(GROUP))

    def code_part(h):
        def step(i, ready):
            peers = group_of(i)
            code_tiles(h, peers)
            for peer in ready:
                send_tile(h, peer)
            return peers

        first = group_of(0)
        code_tiles(h, first)
        ready = lax.fori_loop(1, devices // GROUP, step, first)
        tiles[h][me] = out_b[h, me]
        unit_in[h][me] = unit_out[h, me]
        for peer in ready[:-1]:
            send_tile(h, peer)

    for h in range(PARTS):
        wait_all(in_a[h], h, a_recv)
        if h == PARTS - 1:
            middle_stage()
        code_part(h)
    for h in range(PARTS):
        wait_all(out_a.at[h], h, a_send)

    def arrived(h):
        wait_all(out_b.at[h], h, b_send)
        wait_all(tiles[h], h, b_recv)
        wait_all(unit_out.at[h], h, c_send)
        wait_all(unit_in[h], h, c_recv)

    def right_hand_side(h):
        rows_of = pl.ds(h * part, part)

        def add_tiles(i, running):
            places = [i * GROUP + j for j in range(GROUP)]
            spots = [jnp.clip(table[0, j], 0, slots - 1) for j in places]
            terms = [
                tiles[h][spot].astype(jnp.int32).astype(F32) * unit_in[h][spot] for spot in spots
            ]
            for j, term in zip(places, terms):
                running = running * table[1, j].astype(F32) + term
                red[j, rows_of] = running
            return running

        lax.fori_loop(0, slots // GROUP, add_tiles, jnp.zeros((part, rows), F32))

        @pl.loop(0, count // 2)
        def _(i):
            for g in (2 * i, 2 * i + 1):
                last = jnp.clip(table[2, g], 0, slots - 1)
                res[0, g, rows_of] = red[last, rows_of] * table[3, g].astype(F32)

    for h in range(PARTS):
        arrived(h)
        right_hand_side(h)

    theta = finish()
    theta = jnp.sum(jnp.sum(theta, axis=0, keepdims=True), axis=1, keepdims=True)
    inv[...] = jnp.broadcast_to((1.0 * devices * count * rows) / theta, inv.shape)

    def precondition(blocks, k, fields):
        outs = [
            product(stacked(field), wp[g], values) + field * diag_p[g]
            for g, field in zip(blocks, fields)
        ]
        for g, out in zip(blocks, outs):
            red[k * count + g] = out
            xs[k % 2, g + 1] = stacked(out)

    def apply_blocks(blocks, k, operands):
        fields = [red[k * count + g] for g in blocks]
        nows = [res[k, g] for g in blocks]
        befores = [res[k - 1, g] for g in blocks] if k > 0 else None
        images = [
            product(operand, wa[g], values) + field * diag_a[g]
            for g, field, operand in zip(blocks, fields, operands)
        ]
        laters = [now - image * inv[0:1] for now, image in zip(nows, images)]
        steps = [now - later for now, later in zip(nows, laters)]

        def dots(slot, left, right):
            acc[slot] += sum(a * b for a, b in zip(left, right))

        if k + 1 < STEPS:
            precondition(blocks, k + 1, laters)
        for g, later in zip(blocks, laters):
            res[k + 1, g] = later
        if k == 0:
            dots(0, fields, steps)
        else:
            dots(2 * k - 1, fields, [x - y for x, y in zip(befores, nows)])
            dots(2 * k, fields, steps)
        if k == 2:
            dots(5, [red[g] for g in blocks], laters)
            dots(6, [red[count + g] for g in blocks], laters)
            dots(7, fields, laters)

    def inner(g, k, width):
        near = [xs[k % 2, g + i] for i in range(width + 2)]
        apply_blocks(
            tuple(g + i for i in range(width)),
            k,
            [
                jnp.concatenate([near[i + 1], near[i + 2], near[i]], axis=1)
                for i in range(width)
            ],
        )

    def inners(start, stop, k):
        whole = (stop - start) // BATCH

        @pl.loop(0, whole)
        def _(i):
            inner(start + BATCH * i, k, BATCH)

        if (stop - start) % BATCH:
            inner(start + BATCH * whole, k, (stop - start) % BATCH)

    def preconditions(start, stop):
        whole = (stop - start) // BATCH

        def some(g, width):
            blocks = tuple(g + i for i in range(width))
            precondition(blocks, 0, [res[0, block] for block in blocks])

        @pl.loop(0, whole)
        def _(i):
            some(start + BATCH * i, BATCH)

        if (stop - start) % BATCH:
            some(start + BATCH * whole, (stop - start) % BATCH)

    def halo_copy(k, side):
        return pltpu.make_async_remote_copy(
            src_ref=xs.at[k % 2, count if side == 0 else 1],
            dst_ref=halo.at[k, side],
            send_sem=halo_send.at[k, side],
            recv_sem=halo_recv.at[k, side],
            device_id=after_id if side == 0 else before_id,
            device_id_type=MESH,
        )

    edges = (0, count - 1)
    middle = count // 2 + 1
    acc[...] = jnp.zeros_like(acc)
    precondition(edges, 0, [res[0, g] for g in edges])
    preconditions(1, 9)
    halo_copy(0, 0).start()
    halo_copy(0, 1).start()
    preconditions(9, count - 1)

    link_copy.wait()
    for k in range(STEPS):
        inners(1, middle, k)
        halo_copy(k, 0).wait()
        halo_copy(k, 1).wait()
        buf = k % 2
        apply_blocks(
            edges,
            k,
            [
                jnp.concatenate([xs[buf, 1], xs[buf, 2], halo[k, 0]], axis=1),
                jnp.concatenate([xs[buf, count], halo[k, 1], xs[buf, count - 1]], axis=1),
            ],
        )
        inners(middle, middle + 4, k)
        if k + 1 < STEPS:
            halo_copy(k + 1, 0).start()
            halo_copy(k + 1, 1).start()
        inners(middle + 4, count - 1, k)

    lane = lax.broadcasted_iota(jnp.int32, (values, rows), 1)
    packed = jnp.zeros((values, rows), F32)
    for j in range(8):
        packed = packed + jnp.where(lane == j, jnp.sum(acc[j], axis=1, keepdims=True), 0.0)
    packed = jnp.concatenate([packed, jnp.zeros((rows - values, rows), F32)], axis=0)
    begin, middle_stage, finish = reduce_over(1, packed.T[0:8])
    begin()
    middle_stage()
    total = finish()

    def over(top, bottom):
        usable = bottom != 0.0
        return jnp.where(usable, top / jnp.where(usable, bottom, 1.0), 0.0)

    g00, g10, g11, g21, g22 = (total[j : j + 1] for j in range(5))
    h0, h1, h2 = (-total[j : j + 1] for j in range(5, 8))
    l1, l2 = over(g10, g00), over(g11, g00)
    d1 = g11 - l1 * g10
    mix = g21 - l2 * g10
    l3 = over(mix, d1)
    d2 = g22 - l2 * g11 - l3 * mix
    y1 = h1 - l1 * h0
    y2 = h2 - l2 * h0 - l3 * y1
    e2 = over(y2, d2)
    e1 = over(y1, d1) - l3 * e2
    e0 = over(h0, g00) - l1 * e1 - l2 * e2
    weights = jnp.concatenate([e0, e1, e2, jnp.zeros((rows - 3, rows), F32)], axis=0).T
    e0 = jnp.broadcast_to(weights[0:values, 0:1], (values, rows))
    e1 = jnp.broadcast_to(weights[0:values, 1:2], (values, rows))
    e2 = jnp.broadcast_to(weights[0:values, 2:3], (values, rows))
    scale = inv[0:1]
    for j, factor in enumerate(
        ((1.0 - e0) * scale, (1.0 - e1) * scale, (1.0 - e2) * scale, e0, e1 - e0, e2 - e1, 1.0 - e2)
    ):
        mix_ref[j] = factor


def combine_kernel(res, red, mix_ref, x_hbm, res_hbm, x_all, r_all, sems):
    count, values, rows = x_all.shape
    x0, x1, x2, r0, r1, r2, r3 = (mix_ref[j] for j in range(7))
    pieces = count // PIECE

    def puts(piece):
        part = pl.ds(piece * PIECE, PIECE)
        return (
            pltpu.make_async_copy(x_all.at[part], x_hbm.at[part], sems.at[0, piece]),
            pltpu.make_async_copy(r_all.at[part], res_hbm.at[part], sems.at[1, piece]),
        )

    @pl.loop(0, pieces)
    def _(piece):
        @pl.loop(0, PIECE // 2)
        def _(i):
            for j in range(2):
                g = piece * PIECE + 2 * i + j
                x_all[g] = x0 * red[g] + x1 * red[count + g] + x2 * red[2 * count + g]
                r_all[g] = r0 * res[0, g] + r1 * res[1, g] + r2 * res[2, g] + r3 * res[3, g]

        for put in puts(piece):
            put.start()

    @pl.loop(0, pieces)
    def _(piece):
        for put in puts(piece):
            put.wait()


def mass_solve(target, links, pick, live, relay, history, mixed, mass_diag, mass_next, precond):
    doms, subs = lax.axis_size("dom"), lax.axis_size("sub")
    slots = mixed.shape[0]
    blocks, values, rows = history.shape
    count = mass_diag.shape[0]
    shape = (doms, subs, count, values, rows, slots)

    def kernel(*refs):
        solve_kernel(shape, *refs)

    smem = pl.BlockSpec(memory_space=pltpu.SMEM)
    hbm = pl.BlockSpec(memory_space=pl.ANY)
    field = jax.ShapeDtypeStruct((count, values, rows), F32)
    dma = pltpu.SemaphoreType.DMA
    vmem = pl.BlockSpec(memory_space=pltpu.VMEM)
    parts = (
        pltpu.VMEM((STEPS + 1, count, values, rows), F32),
        pltpu.VMEM((STEPS * count, values, rows), F32),
        pltpu.VMEM((7, values, rows), F32),
    )
    parts = pl.pallas_call(
        kernel,
        out_shape=parts,
        in_specs=[pl.BlockSpec(memory_space=pltpu.VMEM)] + [smem] * 4 + [hbm] * 5,
        out_specs=(vmem,) * 3,
        scratch_shapes=[
            pltpu.VMEM((blocks, values, rows), BF16),
            pltpu.VMEM((slots, rows, rows), BF16),
            pltpu.VMEM((PARTS, slots, values // PARTS, rows), BF16),
            pltpu.VMEM((slots, values // PARTS, rows), BF16),
            pltpu.VMEM((slots, values // PARTS, rows), BF16),
            pltpu.VMEM((PARTS, slots, values // PARTS, rows), jnp.int16),
            pltpu.VMEM((slots, values // PARTS, rows), jnp.int16),
            pltpu.VMEM((slots, values // PARTS, rows), jnp.int16),
            pltpu.VMEM((PARTS, slots, 1, rows), F32),
            pltpu.VMEM((slots, 1, rows), F32),
            pltpu.VMEM((slots, 1, rows), F32),
            pltpu.VMEM((2, 3, CHUNK, rows, rows), F32),
            pltpu.VMEM((count + 1, 3 * rows, 2 * rows), BF16),
            pltpu.VMEM((count, rows, 2 * rows), BF16),
            pltpu.VMEM((count, 1, rows), F32),
            pltpu.VMEM((count, 1, rows), F32),
            pltpu.VMEM((2, count + 2, 2 * values, rows), BF16),
            pltpu.VMEM((STEPS, 2, 2 * values, rows), BF16),
            pltpu.VMEM((8, values, rows), F32),
            pltpu.VMEM((8, rows), F32),
            pltpu.VMEM((8, rows), F32),
            pltpu.VMEM((2, 2, 8, rows), F32),
            pltpu.VMEM((2, doms, 8, rows), F32),
            pltpu.VMEM((2, subs, 8, rows), F32),
            pltpu.VMEM((8, rows), jnp.int32),
            pltpu.SMEM((8, rows), jnp.int32),
            dma,
            pltpu.SemaphoreType.REGULAR((2,)),
            dma,
            dma,
            dma((PARTS,)),
            dma((PARTS,)),
            dma((PARTS,)),
            dma((PARTS,)),
            dma((PARTS,)),
            dma((PARTS,)),
            dma((2, 3)),
            dma((STEPS, 2)),
            dma((STEPS, 2)),
            dma,
            dma,
            dma((2, doms)),
            dma((2, doms)),
            dma((2, subs)),
            dma((2, subs)),
        ],
        compiler_params=pltpu.CompilerParams(
            collective_id=0, has_side_effects=True, vmem_limit_bytes=LIMIT1 * 1024
        ),
    )(target, links, pick, live, relay, history, mixed, mass_diag, mass_next, precond)
    return pl.pallas_call(
        combine_kernel,
        out_shape=(field, field),
        in_specs=[vmem] * 3,
        out_specs=(hbm, hbm),
        scratch_shapes=[
            pltpu.VMEM((count, values, rows), F32),
            pltpu.VMEM((count, values, rows), F32),
            dma((2, count // PIECE)),
        ],
        compiler_params=pltpu.CompilerParams(vmem_limit_bytes=LIMIT2 * 1024),
    )(*parts)


def body(
    history,
    send_list,
    send_count,
    mixed_mass,
    relay_list,
    relay_target,
    mass_diag,
    mass_next,
    coupling,
    precond,
):
    return mass_solve(
        relay_target.reshape(1, -1),
        coupling,
        send_list.reshape(-1),
        send_count.reshape(-1),
        relay_list.reshape(-1),
        history,
        mixed_mass,
        mass_diag,
        mass_next,
        precond,
    )


def solution(mesh):
    whole = ("dom", "sub")
    placed = (
        P(whole, None, None),
        P(whole, None, None),
        P(whole, None),
        P(whole, None, None),
        P(whole, None, None),
        P(whole, None, None),
        P(whole, None, None),
        P(whole, None, None),
        P(whole),
        P(whole, None, None),
    )
    return jax.shard_map(
        body,
        mesh=mesh,
        in_specs=placed,
        out_specs=(P(whole, None, None), P(whole, None, None)),
        check_vma=False,
    )
```

```python
import jax
import jax.numpy as jnp
from jax import lax
from jax.experimental import pallas as pl
from jax.experimental.pallas import tpu as pltpu
from jax.sharding import PartitionSpec as P

MESH = pl.DeviceIdType.MESH
F32 = jnp.float32
BF16 = jnp.bfloat16
STEPS = 3
CHUNK = 4
ORDER = 37
GROUP = 8
PARTS = 2
SMALLEST = 1e-30
PIECE = 8
SUBLANES = 8
LIMIT1 = 46000
LIMIT2 = 8000
BATCH = 8
LEVELS = 32767.0
FIRST_BITS = 0b0101010


def split(value):
    high = value.astype(BF16)
    low = (value - high.astype(F32)).astype(BF16)
    return high, low


def stacked(value):
    return jnp.concatenate(split(value), axis=0)


def product(left, weights, half):
    full = jnp.dot(left, weights, preferred_element_type=F32)
    top = full[:half] + full[half:]
    width = top.shape[1] // 2
    return top[:, :width] + top[:, width:]


def solve_kernel(
    shape,
    target_ref,
    links_ref,
    pick_ref,
    live_ref,
    relay_ref,
    hist_hbm,
    mixed_hbm,
    diag_hbm,
    next_hbm,
    prec_hbm,
    res,
    red,
    mix_ref,
    hist,
    mixed,
    out_a,
    in_a_0,
    in_a_1,
    out_b,
    tiles_0,
    tiles_1,
    unit_out,
    unit_in_0,
    unit_in_1,
    stage,
    wa,
    wp,
    diag_a,
    diag_p,
    xs,
    halo,
    acc,
    trace,
    inv,
    red_src,
    red_dom,
    red_sub,
    rank_rows,
    table,
    table_sem,
    enter,
    hist_sem,
    mixed_sem,
    a_send,
    a_recv,
    b_send,
    b_recv,
    c_send,
    c_recv,
    stage_sem,
    halo_send,
    halo_recv,
    link_send,
    link_recv,
    dom_send,
    dom_recv,
    sub_send,
    sub_recv,
):
    doms, subs, count, values, rows, slots = shape
    devices = doms * subs
    part = values // PARTS
    in_a, tiles, unit_in = (in_a_0, in_a_1), (tiles_0, tiles_1), (unit_in_0, unit_in_1)
    me_dom, me_sub = lax.axis_index("dom"), lax.axis_index("sub")
    me = me_dom * subs + me_sub
    after = lax.rem(me + 1, devices)
    before = lax.rem(me + devices - 1, devices)
    after_id = (after // subs, lax.rem(after, subs))
    before_id = (before // subs, lax.rem(before, subs))

    load_hist = pltpu.make_async_copy(hist_hbm, hist, hist_sem)
    load_hist.start()
    load_mixed = pltpu.make_async_copy(mixed_hbm, mixed, mixed_sem)

    def peer_of(s):
        place = (s * ORDER) & (devices - 1)
        carry = (place & me & FIRST_BITS) << 1
        return place ^ me ^ carry

    def id_of(peer):
        return (peer >> 3, peer & (subs - 1))

    width = 4
    me_y, me_x = me_dom >> 2, me_dom & (width - 1)

    def line_x(j):
        return (me_y * width + ((me_x + j) & (width - 1)), me_sub)

    def line_y(j):
        return (((me_y + j) & (width - 1)) * width + me_x, me_sub)

    barrier = pltpu.get_barrier_semaphore()
    for j in range(1, subs):
        other = (me_dom, (me_sub + j) & (subs - 1))
        pl.semaphore_signal(barrier, inc=1, device_id=other, device_id_type=MESH)
    for j in range(1, width):
        pl.semaphore_signal(barrier, inc=1, device_id=line_x(j), device_id_type=MESH)
        pl.semaphore_signal(barrier, inc=1, device_id=line_y(j), device_id_type=MESH)

    pl.semaphore_wait(barrier, subs - 1 + 2 * (width - 1))
    for j in range(1, width):
        pl.semaphore_signal(enter.at[0], inc=1, device_id=line_x(j), device_id_type=MESH)
    pl.semaphore_wait(enter.at[0], width - 1)
    for j in range(1, width):
        pl.semaphore_signal(enter.at[1], inc=1, device_id=line_y(j), device_id_type=MESH)

    load_hist.wait()

    @pl.loop(0, devices)
    def _(e):
        block = hist[pick_ref[e]]
        block = jnp.where(live_ref[e] > 0, block, jnp.zeros_like(block))
        for h in range(PARTS):
            out_a[h, e] = block[h * part : (h + 1) * part]

    pl.semaphore_wait(enter.at[1], width - 1)

    for h in range(PARTS):

        @pl.loop(1, devices)
        def _(s):
            peer = peer_of(s)
            pltpu.make_async_remote_copy(
                src_ref=out_a.at[h, peer],
                dst_ref=in_a[h].at[me],
                send_sem=a_send.at[h],
                recv_sem=a_recv.at[h],
                device_id=id_of(peer),
                device_id_type=MESH,
            ).start()

    for h in range(PARTS):
        in_a[h][me] = out_a[h, me]
    load_mixed.start()

    spot = lax.broadcasted_iota(jnp.int32, (slots, slots), 0)
    place = lax.broadcasted_iota(jnp.int32, (slots, slots), 1)
    target = jnp.broadcast_to(target_ref[...], (slots, slots))
    target_of = jnp.sum(jnp.where(spot == place, target, 0), axis=1, keepdims=True)
    earlier = target * slots + place < target_of * slots + spot
    rank = jnp.sum(earlier.astype(jnp.int32), axis=1, keepdims=True)
    chosen = rank == place
    order = jnp.sum(jnp.where(chosen, spot, 0), axis=0, keepdims=True)
    ordered = jnp.sum(jnp.where(chosen, target_of, 0), axis=0, keepdims=True)
    shifted = pltpu.roll(ordered, 1, 1)
    same = jnp.where((shifted == ordered) & (place[0:1] > 0), 1, 0)
    upto = jnp.sum((target_of <= place).astype(jnp.int32), axis=0, keepdims=True)
    here = jnp.sum((target_of == place).astype(jnp.int32), axis=0, keepdims=True)
    rank_rows[0:1] = order
    rank_rows[1:2] = same
    rank_rows[2:3] = jnp.maximum(upto - 1, 0)
    rank_rows[3:4] = jnp.where(here > 0, 1, 0)
    rank_rows[4:8] = jnp.zeros((4, rows), jnp.int32)
    load_table = pltpu.make_async_copy(rank_rows, table, table_sem)
    load_table.start()

    sources = (diag_hbm, next_hbm, prec_hbm)

    def stage_copy(chunk, which):
        slot = lax.rem(chunk, 2)
        return pltpu.make_async_copy(
            sources[which].at[pl.ds(chunk * CHUNK, CHUNK)],
            stage.at[slot, which],
            stage_sem.at[slot, which],
        )

    for which in range(3):
        stage_copy(0, which).start()
    trace[...] = jnp.zeros_like(trace)
    row = lax.broadcasted_iota(jnp.int32, (rows, rows), 0)
    col = lax.broadcasted_iota(jnp.int32, (rows, rows), 1)
    eye = row == col
    chunks = count // CHUNK

    @pl.loop(0, chunks)
    def _(chunk):
        @pl.when(chunk + 1 < chunks)
        def _():
            for which in range(3):
                stage_copy(chunk + 1, which).start()

        for which in range(3):
            stage_copy(chunk, which).wait()
        slot = lax.rem(chunk, 2)

        @pl.loop(0, CHUNK)
        def _(i):
            g = chunk * CHUNK + i
            here = stage[slot, 0, i]
            onto = stage[slot, 1, i]
            prec = stage[slot, 2, i]
            trace[...] += jnp.sum((here * prec).reshape(rows // 8, 8, rows), axis=0)
            diag_a[g] = jnp.sum(jnp.where(eye, here, 0.0), axis=0, keepdims=True)
            diag_p[g] = jnp.sum(jnp.where(eye, prec, 0.0), axis=0, keepdims=True)
            high, low = split(jnp.where(eye, 0.0, here))
            wa[g, 0:rows, 0:rows] = high
            wa[g, 0:rows, rows : 2 * rows] = low
            wrap = jnp.logical_and(g == count - 1, me == devices - 1)
            link = jnp.where(wrap, 0.0, links_ref[g].astype(F32))
            onto = onto * link
            high, low = split(onto)
            wa[g + 1, 2 * rows : 3 * rows, 0:rows] = high
            wa[g + 1, 2 * rows : 3 * rows, rows : 2 * rows] = low
            high, low = split(onto.T)
            wa[g, rows : 2 * rows, 0:rows] = high
            wa[g, rows : 2 * rows, rows : 2 * rows] = low
            high, low = split(jnp.where(eye, 0.0, prec))
            wp[g, :, 0:rows] = high
            wp[g, :, rows : 2 * rows] = low

    def reduce_over(phase, value):
        def dom_copy(peer, slot):
            return pltpu.make_async_remote_copy(
                src_ref=red_src.at[phase, 0],
                dst_ref=red_dom.at[phase, slot],
                send_sem=dom_send.at[phase, peer],
                recv_sem=dom_recv.at[phase, slot],
                device_id=(peer, me_sub),
                device_id_type=MESH,
            )

        def sub_copy(peer, slot):
            return pltpu.make_async_remote_copy(
                src_ref=red_src.at[phase, 1],
                dst_ref=red_sub.at[phase, slot],
                send_sem=sub_send.at[phase, peer],
                recv_sem=sub_recv.at[phase, slot],
                device_id=(me_dom, peer),
                device_id_type=MESH,
            )

        def begin():
            red_src[phase, 0] = value
            red_dom[phase, me_dom] = value

            for j in range(1, doms):
                dom_copy((me_dom + j) & (doms - 1), me_dom).start()

        def middle_stage():
            for j in range(1, doms):
                other = (me_dom + j) & (doms - 1)
                dom_copy(other, other).wait_recv()

            total = red_dom[phase, 0]
            for j in range(1, doms):
                total = total + red_dom[phase, j]
            red_src[phase, 1] = total
            red_sub[phase, me_sub] = total

            for j in range(1, subs):
                sub_copy((me_sub + j) & (subs - 1), me_sub).start()

        def finish():
            for j in range(1, subs):
                other = (me_sub + j) & (subs - 1)
                sub_copy(other, other).wait_recv()

            total = red_sub[phase, 0]
            for j in range(1, subs):
                total = total + red_sub[phase, j]

            for j in range(1, doms):
                dom_copy((me_dom + j) & (doms - 1), me_dom).wait_send()

            for j in range(1, subs):
                sub_copy((me_sub + j) & (subs - 1), me_sub).wait_send()

            return total

        return begin, middle_stage, finish

    link_copy = pltpu.make_async_remote_copy(
        src_ref=wa.at[count, pl.ds(2 * rows, rows)],
        dst_ref=wa.at[0, pl.ds(2 * rows, rows)],
        send_sem=link_send,
        recv_sem=link_recv,
        device_id=after_id,
        device_id_type=MESH,
    )
    link_copy.start()
    begin, middle_stage, finish = reduce_over(0, trace[...])
    begin()
    load_table.wait()

    others = pl.ds(0, devices - 1)
    load_mixed.wait()

    def wait_all(buffer, h, semaphore):
        view = buffer.at[others]
        pltpu.make_async_copy(view, view, semaphore.at[h]).wait()

    def code_tiles(h, peers):
        spots = [relay_ref[peer] for peer in peers]
        values_of = [
            jnp.dot(in_a[h][spot], mixed[spot], preferred_element_type=F32) for spot in spots
        ]
        tops = [jnp.max(jnp.abs(tile), axis=(0, 1), keepdims=True) for tile in values_of]
        units = [jnp.maximum(top, SMALLEST) / LEVELS for top in tops]
        codes = [jnp.round(tile * (1.0 / unit)) for tile, unit in zip(values_of, units)]
        for peer, code, unit in zip(peers, codes, units):
            out_b[h, peer] = code.astype(jnp.int32).astype(jnp.int16)
            unit_out[h, peer] = jnp.broadcast_to(unit, (1, rows))

    def send_tile(h, peer):
        for source, target, send, receive in (
            (out_b, tiles, b_send, b_recv),
            (unit_out, unit_in, c_send, c_recv),
        ):
            pltpu.make_async_remote_copy(
                src_ref=source.at[h, peer],
                dst_ref=target[h].at[me],
                send_sem=send.at[h],
                recv_sem=receive.at[h],
                device_id=id_of(peer),
                device_id_type=MESH,
            ).start()

    def group_of(i):
        return tuple(peer_of(i * GROUP + 1 + j) for j in range(GROUP))

    def code_part(h):
        def step(i, ready):
            peers = group_of(i)
            code_tiles(h, peers)
            for peer in ready:
                send_tile(h, peer)
            return peers

        first = group_of(0)
        code_tiles(h, first)
        ready = lax.fori_loop(1, devices // GROUP, step, first)
        tiles[h][me] = out_b[h, me]
        unit_in[h][me] = unit_out[h, me]
        for peer in ready[:-1]:
            send_tile(h, peer)

    for h in range(PARTS):
        wait_all(in_a[h], h, a_recv)
        if h == PARTS - 1:
            middle_stage()
        code_part(h)
    for h in range(PARTS):
        wait_all(out_a.at[h], h, a_send)

    def arrived(h):
        wait_all(out_b.at[h], h, b_send)
        wait_all(tiles[h], h, b_recv)
        wait_all(unit_out.at[h], h, c_send)
        wait_all(unit_in[h], h, c_recv)

    def right_hand_side(h):
        rows_of = pl.ds(h * part, part)

        def add_tiles(i, running):
            places = [i * GROUP + j for j in range(GROUP)]
            spots = [jnp.clip(table[0, j], 0, slots - 1) for j in places]
            terms = [
                tiles[h][spot].astype(jnp.int32).astype(F32) * unit_in[h][spot] for spot in spots
            ]
            for j, term in zip(places, terms):
                running = running * table[1, j].astype(F32) + term
                red[j, rows_of] = running
            return running

        lax.fori_loop(0, slots // GROUP, add_tiles, jnp.zeros((part, rows), F32))

        @pl.loop(0, count // 2)
        def _(i):
            for g in (2 * i, 2 * i + 1):
                last = jnp.clip(table[2, g], 0, slots - 1)
                res[0, g, rows_of] = red[last, rows_of] * table[3, g].astype(F32)

    for h in range(PARTS):
        arrived(h)
        right_hand_side(h)

    theta = finish()
    theta = jnp.sum(jnp.sum(theta, axis=0, keepdims=True), axis=1, keepdims=True)
    inv[...] = jnp.broadcast_to((1.0 * devices * count * rows) / theta, inv.shape)

    def precondition(blocks, k, fields):
        outs = [
            product(stacked(field), wp[g], values) + field * diag_p[g]
            for g, field in zip(blocks, fields)
        ]
        for g, out in zip(blocks, outs):
            red[k * count + g] = out
            xs[k % 2, g + 1] = stacked(out)

    def apply_blocks(blocks, k, operands):
        fields = [red[k * count + g] for g in blocks]
        nows = [res[k, g] for g in blocks]
        befores = [res[k - 1, g] for g in blocks] if k > 0 else None
        images = [
            product(operand, wa[g], values) + field * diag_a[g]
            for g, field, operand in zip(blocks, fields, operands)
        ]
        laters = [now - image * inv[0:1] for now, image in zip(nows, images)]
        steps = [now - later for now, later in zip(nows, laters)]

        def dots(slot, left, right):
            acc[slot] += sum(a * b for a, b in zip(left, right))

        if k + 1 < STEPS:
            precondition(blocks, k + 1, laters)
        for g, later in zip(blocks, laters):
            res[k + 1, g] = later
        if k == 0:
            dots(0, fields, steps)
        else:
            dots(2 * k - 1, fields, [x - y for x, y in zip(befores, nows)])
            dots(2 * k, fields, steps)
        if k == 2:
            dots(5, [red[g] for g in blocks], laters)
            dots(6, [red[count + g] for g in blocks], laters)
            dots(7, fields, laters)

    def inner(g, k, width):
        near = [xs[k % 2, g + i] for i in range(width + 2)]
        apply_blocks(
            tuple(g + i for i in range(width)),
            k,
            [
                jnp.concatenate([near[i + 1], near[i + 2], near[i]], axis=1)
                for i in range(width)
            ],
        )

    def inners(start, stop, k):
        whole = (stop - start) // BATCH

        @pl.loop(0, whole)
        def _(i):
            inner(start + BATCH * i, k, BATCH)

        if (stop - start) % BATCH:
            inner(start + BATCH * whole, k, (stop - start) % BATCH)

    def preconditions(start, stop):
        whole = (stop - start) // BATCH

        def some(g, width):
            blocks = tuple(g + i for i in range(width))
            precondition(blocks, 0, [res[0, block] for block in blocks])

        @pl.loop(0, whole)
        def _(i):
            some(start + BATCH * i, BATCH)

        if (stop - start) % BATCH:
            some(start + BATCH * whole, (stop - start) % BATCH)

    def halo_copy(k, side):
        return pltpu.make_async_remote_copy(
            src_ref=xs.at[k % 2, count if side == 0 else 1],
            dst_ref=halo.at[k, side],
            send_sem=halo_send.at[k, side],
            recv_sem=halo_recv.at[k, side],
            device_id=after_id if side == 0 else before_id,
            device_id_type=MESH,
        )

    edges = (0, count - 1)
    middle = count // 2 + 1
    acc[...] = jnp.zeros_like(acc)
    precondition(edges, 0, [res[0, g] for g in edges])
    preconditions(1, 9)
    halo_copy(0, 0).start()
    halo_copy(0, 1).start()
    preconditions(9, count - 1)

    link_copy.wait()
    for k in range(STEPS):
        inners(1, middle, k)
        halo_copy(k, 0).wait()
        halo_copy(k, 1).wait()
        buf = k % 2
        apply_blocks(
            edges,
            k,
            [
                jnp.concatenate([xs[buf, 1], xs[buf, 2], halo[k, 0]], axis=1),
                jnp.concatenate([xs[buf, count], halo[k, 1], xs[buf, count - 1]], axis=1),
            ],
        )
        inners(middle, middle + 4, k)
        if k + 1 < STEPS:
            halo_copy(k + 1, 0).start()
            halo_copy(k + 1, 1).start()
        inners(middle + 4, count - 1, k)

    lane = lax.broadcasted_iota(jnp.int32, (values, rows), 1)
    packed = jnp.zeros((values, rows), F32)
    for j in range(8):
        packed = packed + jnp.where(lane == j, jnp.sum(acc[j], axis=1, keepdims=True), 0.0)
    packed = jnp.concatenate([packed, jnp.zeros((rows - values, rows), F32)], axis=0)
    begin, middle_stage, finish = reduce_over(1, packed.T[0:8])
    begin()
    middle_stage()
    total = finish()

    def over(top, bottom):
        usable = bottom != 0.0
        return jnp.where(usable, top / jnp.where(usable, bottom, 1.0), 0.0)

    g00, g10, g11, g21, g22 = (total[j : j + 1] for j in range(5))
    h0, h1, h2 = (-total[j : j + 1] for j in range(5, 8))
    l1, l2 = over(g10, g00), over(g11, g00)
    d1 = g11 - l1 * g10
    mix = g21 - l2 * g10
    l3 = over(mix, d1)
    d2 = g22 - l2 * g11 - l3 * mix
    y1 = h1 - l1 * h0
    y2 = h2 - l2 * h0 - l3 * y1
    e2 = over(y2, d2)
    e1 = over(y1, d1) - l3 * e2
    e0 = over(h0, g00) - l1 * e1 - l2 * e2
    weights = jnp.concatenate([e0, e1, e2, jnp.zeros((rows - 3, rows), F32)], axis=0).T
    e0 = jnp.broadcast_to(weights[0:values, 0:1], (values, rows))
    e1 = jnp.broadcast_to(weights[0:values, 1:2], (values, rows))
    e2 = jnp.broadcast_to(weights[0:values, 2:3], (values, rows))
    scale = inv[0:1]
    for j, factor in enumerate(
        ((1.0 - e0) * scale, (1.0 - e1) * scale, (1.0 - e2) * scale, e0, e1 - e0, e2 - e1, 1.0 - e2)
    ):
        mix_ref[j] = factor


def combine_kernel(res, red, mix_ref, x_hbm, res_hbm, x_all, r_all, sems):
    count, values, rows = x_all.shape
    pieces = count // PIECE

    def puts(piece):
        part = pl.ds(piece * PIECE, PIECE)
        return (
            pltpu.make_async_copy(x_all.at[part], x_hbm.at[part], sems.at[0, piece]),
            pltpu.make_async_copy(r_all.at[part], res_hbm.at[part], sems.at[1, piece]),
        )

    @pl.loop(0, pieces)
    def _(piece):
        for top in range(0, values, SUBLANES):
            some = pl.ds(top, SUBLANES)
            x0, x1, x2, r0, r1, r2, r3 = (mix_ref[j, some] for j in range(7))
            for i in range(PIECE):
                g = piece * PIECE + i
                x_all[g, some] = (
                    x0 * red[g, some] + x1 * red[count + g, some] + x2 * red[2 * count + g, some]
                )
                r_all[g, some] = (
                    r0 * res[0, g, some]
                    + r1 * res[1, g, some]
                    + r2 * res[2, g, some]
                    + r3 * res[3, g, some]
                )

        for put in puts(piece):
            put.start()

    @pl.loop(0, pieces)
    def _(piece):
        for put in puts(piece):
            put.wait()


def mass_solve(target, links, pick, live, relay, history, mixed, mass_diag, mass_next, precond):
    doms, subs = lax.axis_size("dom"), lax.axis_size("sub")
    slots = mixed.shape[0]
    blocks, values, rows = history.shape
    count = mass_diag.shape[0]
    shape = (doms, subs, count, values, rows, slots)

    def kernel(*refs):
        solve_kernel(shape, *refs)

    smem = pl.BlockSpec(memory_space=pltpu.SMEM)
    hbm = pl.BlockSpec(memory_space=pl.ANY)
    field = jax.ShapeDtypeStruct((count, values, rows), F32)
    dma = pltpu.SemaphoreType.DMA
    vmem = pl.BlockSpec(memory_space=pltpu.VMEM)
    parts = (
        pltpu.VMEM((STEPS + 1, count, values, rows), F32),
        pltpu.VMEM((STEPS * count, values, rows), F32),
        pltpu.VMEM((7, values, rows), F32),
    )
    parts = pl.pallas_call(
        kernel,
        out_shape=parts,
        in_specs=[pl.BlockSpec(memory_space=pltpu.VMEM)] + [smem] * 4 + [hbm] * 5,
        out_specs=(vmem,) * 3,
        scratch_shapes=[
            pltpu.VMEM((blocks, values, rows), BF16),
            pltpu.VMEM((slots, rows, rows), BF16),
            pltpu.VMEM((PARTS, slots, values // PARTS, rows), BF16),
            pltpu.VMEM((slots, values // PARTS, rows), BF16),
            pltpu.VMEM((slots, values // PARTS, rows), BF16),
            pltpu.VMEM((PARTS, slots, values // PARTS, rows), jnp.int16),
            pltpu.VMEM((slots, values // PARTS, rows), jnp.int16),
            pltpu.VMEM((slots, values // PARTS, rows), jnp.int16),
            pltpu.VMEM((PARTS, slots, 1, rows), F32),
            pltpu.VMEM((slots, 1, rows), F32),
            pltpu.VMEM((slots, 1, rows), F32),
            pltpu.VMEM((2, 3, CHUNK, rows, rows), F32),
            pltpu.VMEM((count + 1, 3 * rows, 2 * rows), BF16),
            pltpu.VMEM((count, rows, 2 * rows), BF16),
            pltpu.VMEM((count, 1, rows), F32),
            pltpu.VMEM((count, 1, rows), F32),
            pltpu.VMEM((2, count + 2, 2 * values, rows), BF16),
            pltpu.VMEM((STEPS, 2, 2 * values, rows), BF16),
            pltpu.VMEM((8, values, rows), F32),
            pltpu.VMEM((8, rows), F32),
            pltpu.VMEM((8, rows), F32),
            pltpu.VMEM((2, 2, 8, rows), F32),
            pltpu.VMEM((2, doms, 8, rows), F32),
            pltpu.VMEM((2, subs, 8, rows), F32),
            pltpu.VMEM((8, rows), jnp.int32),
            pltpu.SMEM((8, rows), jnp.int32),
            dma,
            pltpu.SemaphoreType.REGULAR((2,)),
            dma,
            dma,
            dma((PARTS,)),
            dma((PARTS,)),
            dma((PARTS,)),
            dma((PARTS,)),
            dma((PARTS,)),
            dma((PARTS,)),
            dma((2, 3)),
            dma((STEPS, 2)),
            dma((STEPS, 2)),
            dma,
            dma,
            dma((2, doms)),
            dma((2, doms)),
            dma((2, subs)),
            dma((2, subs)),
        ],
        compiler_params=pltpu.CompilerParams(
            collective_id=0, has_side_effects=True, vmem_limit_bytes=LIMIT1 * 1024
        ),
    )(target, links, pick, live, relay, history, mixed, mass_diag, mass_next, precond)
    return pl.pallas_call(
        combine_kernel,
        out_shape=(field, field),
        in_specs=[vmem] * 3,
        out_specs=(hbm, hbm),
        scratch_shapes=[
            pltpu.VMEM((count, values, rows), F32),
            pltpu.VMEM((count, values, rows), F32),
            dma((2, count // PIECE)),
        ],
        compiler_params=pltpu.CompilerParams(vmem_limit_bytes=LIMIT2 * 1024),
    )(*parts)


def body(
    history,
    send_list,
    send_count,
    mixed_mass,
    relay_list,
    relay_target,
    mass_diag,
    mass_next,
    coupling,
    precond,
):
    return mass_solve(
        relay_target.reshape(1, -1),
        coupling,
        send_list.reshape(-1),
        send_count.reshape(-1),
        relay_list.reshape(-1),
        history,
        mixed_mass,
        mass_diag,
        mass_next,
        precond,
    )


def solution(mesh):
    whole = ("dom", "sub")
    placed = (
        P(whole, None, None),
        P(whole, None, None),
        P(whole, None),
        P(whole, None, None),
        P(whole, None, None),
        P(whole, None, None),
        P(whole, None, None),
        P(whole, None, None),
        P(whole),
        P(whole, None, None),
    )
    return jax.shard_map(
        body,
        mesh=mesh,
        in_specs=placed,
        out_specs=(P(whole, None, None), P(whole, None, None)),
        check_vma=False,
    )
```

```python
import jax
import jax.numpy as jnp
from jax import lax
from jax.experimental import pallas as pl
from jax.experimental.pallas import tpu as pltpu
from jax.sharding import PartitionSpec as P

MESH = pl.DeviceIdType.MESH
F32 = jnp.float32
BF16 = jnp.bfloat16
STEPS = 3
CHUNK = 4
ORDER = 37
GROUP = 8
PARTS = 2
SMALLEST = 1e-30
PIECE = 8
SUBLANES = 8
LIMIT1 = 46000
LIMIT2 = 8000
BATCH = 16
LEVELS = 32767.0
FIRST_BITS = 0b0101010


def split(value):
    high = value.astype(BF16)
    low = (value - high.astype(F32)).astype(BF16)
    return high, low


def stacked(value):
    return jnp.concatenate(split(value), axis=0)


def product(left, weights, half):
    full = jnp.dot(left, weights, preferred_element_type=F32)
    top = full[:half] + full[half:]
    width = top.shape[1] // 2
    return top[:, :width] + top[:, width:]


def solve_kernel(
    shape,
    target_ref,
    links_ref,
    pick_ref,
    live_ref,
    relay_ref,
    hist_hbm,
    mixed_hbm,
    diag_hbm,
    next_hbm,
    prec_hbm,
    res,
    red,
    mix_ref,
    hist,
    mixed,
    out_a,
    in_a_0,
    in_a_1,
    out_b,
    tiles_0,
    tiles_1,
    unit_out,
    unit_in_0,
    unit_in_1,
    stage,
    wa,
    wp,
    diag_a,
    diag_p,
    xs,
    halo,
    acc,
    trace,
    inv,
    red_src,
    red_dom,
    red_sub,
    rank_rows,
    table,
    table_sem,
    enter,
    hist_sem,
    mixed_sem,
    a_send,
    a_recv,
    b_send,
    b_recv,
    c_send,
    c_recv,
    stage_sem,
    halo_send,
    halo_recv,
    link_send,
    link_recv,
    dom_send,
    dom_recv,
    sub_send,
    sub_recv,
):
    doms, subs, count, values, rows, slots = shape
    devices = doms * subs
    part = values // PARTS
    in_a, tiles, unit_in = (in_a_0, in_a_1), (tiles_0, tiles_1), (unit_in_0, unit_in_1)
    me_dom, me_sub = lax.axis_index("dom"), lax.axis_index("sub")
    me = me_dom * subs + me_sub
    after = lax.rem(me + 1, devices)
    before = lax.rem(me + devices - 1, devices)
    after_id = (after // subs, lax.rem(after, subs))
    before_id = (before // subs, lax.rem(before, subs))

    load_hist = pltpu.make_async_copy(hist_hbm, hist, hist_sem)
    load_hist.start()
    load_mixed = pltpu.make_async_copy(mixed_hbm, mixed, mixed_sem)

    def peer_of(s):
        place = (s * ORDER) & (devices - 1)
        carry = (place & me & FIRST_BITS) << 1
        return place ^ me ^ carry

    def id_of(peer):
        return (peer >> 3, peer & (subs - 1))

    width = 4
    me_y, me_x = me_dom >> 2, me_dom & (width - 1)

    def line_x(j):
        return (me_y * width + ((me_x + j) & (width - 1)), me_sub)

    def line_y(j):
        return (((me_y + j) & (width - 1)) * width + me_x, me_sub)

    barrier = pltpu.get_barrier_semaphore()
    for j in range(1, subs):
        other = (me_dom, (me_sub + j) & (subs - 1))
        pl.semaphore_signal(barrier, inc=1, device_id=other, device_id_type=MESH)
    for j in range(1, width):
        pl.semaphore_signal(barrier, inc=1, device_id=line_x(j), device_id_type=MESH)
        pl.semaphore_signal(barrier, inc=1, device_id=line_y(j), device_id_type=MESH)

    pl.semaphore_wait(barrier, subs - 1 + 2 * (width - 1))
    for j in range(1, width):
        pl.semaphore_signal(enter.at[0], inc=1, device_id=line_x(j), device_id_type=MESH)
    pl.semaphore_wait(enter.at[0], width - 1)
    for j in range(1, width):
        pl.semaphore_signal(enter.at[1], inc=1, device_id=line_y(j), device_id_type=MESH)

    load_hist.wait()

    @pl.loop(0, devices)
    def _(e):
        block = hist[pick_ref[e]]
        block = jnp.where(live_ref[e] > 0, block, jnp.zeros_like(block))
        for h in range(PARTS):
            out_a[h, e] = block[h * part : (h + 1) * part]

    pl.semaphore_wait(enter.at[1], width - 1)

    for h in range(PARTS):

        @pl.loop(1, devices)
        def _(s):
            peer = peer_of(s)
            pltpu.make_async_remote_copy(
                src_ref=out_a.at[h, peer],
                dst_ref=in_a[h].at[me],
                send_sem=a_send.at[h],
                recv_sem=a_recv.at[h],
                device_id=id_of(peer),
                device_id_type=MESH,
            ).start()

    for h in range(PARTS):
        in_a[h][me] = out_a[h, me]
    load_mixed.start()

    spot = lax.broadcasted_iota(jnp.int32, (slots, slots), 0)
    place = lax.broadcasted_iota(jnp.int32, (slots, slots), 1)
    target = jnp.broadcast_to(target_ref[...], (slots, slots))
    target_of = jnp.sum(jnp.where(spot == place, target, 0), axis=1, keepdims=True)
    earlier = target * slots + place < target_of * slots + spot
    rank = jnp.sum(earlier.astype(jnp.int32), axis=1, keepdims=True)
    chosen = rank == place
    order = jnp.sum(jnp.where(chosen, spot, 0), axis=0, keepdims=True)
    ordered = jnp.sum(jnp.where(chosen, target_of, 0), axis=0, keepdims=True)
    shifted = pltpu.roll(ordered, 1, 1)
    same = jnp.where((shifted == ordered) & (place[0:1] > 0), 1, 0)
    upto = jnp.sum((target_of <= place).astype(jnp.int32), axis=0, keepdims=True)
    here = jnp.sum((target_of == place).astype(jnp.int32), axis=0, keepdims=True)
    rank_rows[0:1] = order
    rank_rows[1:2] = same
    rank_rows[2:3] = jnp.maximum(upto - 1, 0)
    rank_rows[3:4] = jnp.where(here > 0, 1, 0)
    rank_rows[4:8] = jnp.zeros((4, rows), jnp.int32)
    load_table = pltpu.make_async_copy(rank_rows, table, table_sem)
    load_table.start()

    sources = (diag_hbm, next_hbm, prec_hbm)

    def stage_copy(chunk, which):
        slot = lax.rem(chunk, 2)
        return pltpu.make_async_copy(
            sources[which].at[pl.ds(chunk * CHUNK, CHUNK)],
            stage.at[slot, which],
            stage_sem.at[slot, which],
        )

    for which in range(3):
        stage_copy(0, which).start()
    trace[...] = jnp.zeros_like(trace)
    row = lax.broadcasted_iota(jnp.int32, (rows, rows), 0)
    col = lax.broadcasted_iota(jnp.int32, (rows, rows), 1)
    eye = row == col
    chunks = count // CHUNK

    @pl.loop(0, chunks)
    def _(chunk):
        @pl.when(chunk + 1 < chunks)
        def _():
            for which in range(3):
                stage_copy(chunk + 1, which).start()

        for which in range(3):
            stage_copy(chunk, which).wait()
        slot = lax.rem(chunk, 2)

        @pl.loop(0, CHUNK)
        def _(i):
            g = chunk * CHUNK + i
            here = stage[slot, 0, i]
            onto = stage[slot, 1, i]
            prec = stage[slot, 2, i]
            trace[...] += jnp.sum((here * prec).reshape(rows // 8, 8, rows), axis=0)
            diag_a[g] = jnp.sum(jnp.where(eye, here, 0.0), axis=0, keepdims=True)
            diag_p[g] = jnp.sum(jnp.where(eye, prec, 0.0), axis=0, keepdims=True)
            high, low = split(jnp.where(eye, 0.0, here))
            wa[g, 0:rows, 0:rows] = high
            wa[g, 0:rows, rows : 2 * rows] = low
            wrap = jnp.logical_and(g == count - 1, me == devices - 1)
            link = jnp.where(wrap, 0.0, links_ref[g].astype(F32))
            onto = onto * link
            high, low = split(onto)
            wa[g + 1, 2 * rows : 3 * rows, 0:rows] = high
            wa[g + 1, 2 * rows : 3 * rows, rows : 2 * rows] = low
            high, low = split(onto.T)
            wa[g, rows : 2 * rows, 0:rows] = high
            wa[g, rows : 2 * rows, rows : 2 * rows] = low
            high, low = split(jnp.where(eye, 0.0, prec))
            wp[g, :, 0:rows] = high
            wp[g, :, rows : 2 * rows] = low

    def reduce_over(phase, value):
        def dom_copy(peer, slot):
            return pltpu.make_async_remote_copy(
                src_ref=red_src.at[phase, 0],
                dst_ref=red_dom.at[phase, slot],
                send_sem=dom_send.at[phase, peer],
                recv_sem=dom_recv.at[phase, slot],
                device_id=(peer, me_sub),
                device_id_type=MESH,
            )

        def sub_copy(peer, slot):
            return pltpu.make_async_remote_copy(
                src_ref=red_src.at[phase, 1],
                dst_ref=red_sub.at[phase, slot],
                send_sem=sub_send.at[phase, peer],
                recv_sem=sub_recv.at[phase, slot],
                device_id=(me_dom, peer),
                device_id_type=MESH,
            )

        def begin():
            red_src[phase, 0] = value
            red_dom[phase, me_dom] = value

            for j in range(1, doms):
                dom_copy((me_dom + j) & (doms - 1), me_dom).start()

        def middle_stage():
            for j in range(1, doms):
                other = (me_dom + j) & (doms - 1)
                dom_copy(other, other).wait_recv()

            total = red_dom[phase, 0]
            for j in range(1, doms):
                total = total + red_dom[phase, j]
            red_src[phase, 1] = total
            red_sub[phase, me_sub] = total

            for j in range(1, subs):
                sub_copy((me_sub + j) & (subs - 1), me_sub).start()

        def finish():
            for j in range(1, subs):
                other = (me_sub + j) & (subs - 1)
                sub_copy(other, other).wait_recv()

            total = red_sub[phase, 0]
            for j in range(1, subs):
                total = total + red_sub[phase, j]

            for j in range(1, doms):
                dom_copy((me_dom + j) & (doms - 1), me_dom).wait_send()

            for j in range(1, subs):
                sub_copy((me_sub + j) & (subs - 1), me_sub).wait_send()

            return total

        return begin, middle_stage, finish

    link_copy = pltpu.make_async_remote_copy(
        src_ref=wa.at[count, pl.ds(2 * rows, rows)],
        dst_ref=wa.at[0, pl.ds(2 * rows, rows)],
        send_sem=link_send,
        recv_sem=link_recv,
        device_id=after_id,
        device_id_type=MESH,
    )
    link_copy.start()
    begin, middle_stage, finish = reduce_over(0, trace[...])
    begin()
    load_table.wait()

    others = pl.ds(0, devices - 1)
    load_mixed.wait()

    def wait_all(buffer, h, semaphore):
        view = buffer.at[others]
        pltpu.make_async_copy(view, view, semaphore.at[h]).wait()

    def code_tiles(h, peers):
        spots = [relay_ref[peer] for peer in peers]
        values_of = [
            jnp.dot(in_a[h][spot], mixed[spot], preferred_element_type=F32) for spot in spots
        ]
        tops = [jnp.max(jnp.abs(tile), axis=(0, 1), keepdims=True) for tile in values_of]
        units = [jnp.maximum(top, SMALLEST) / LEVELS for top in tops]
        codes = [jnp.round(tile * (1.0 / unit)) for tile, unit in zip(values_of, units)]
        for peer, code, unit in zip(peers, codes, units):
            out_b[h, peer] = code.astype(jnp.int32).astype(jnp.int16)
            unit_out[h, peer] = jnp.broadcast_to(unit, (1, rows))

    def send_tile(h, peer):
        for source, target, send, receive in (
            (out_b, tiles, b_send, b_recv),
            (unit_out, unit_in, c_send, c_recv),
        ):
            pltpu.make_async_remote_copy(
                src_ref=source.at[h, peer],
                dst_ref=target[h].at[me],
                send_sem=send.at[h],
                recv_sem=receive.at[h],
                device_id=id_of(peer),
                device_id_type=MESH,
            ).start()

    def group_of(i):
        return tuple(peer_of(i * GROUP + 1 + j) for j in range(GROUP))

    def code_part(h):
        def step(i, ready):
            peers = group_of(i)
            code_tiles(h, peers)
            for peer in ready:
                send_tile(h, peer)
            return peers

        first = group_of(0)
        code_tiles(h, first)
        ready = lax.fori_loop(1, devices // GROUP, step, first)
        tiles[h][me] = out_b[h, me]
        unit_in[h][me] = unit_out[h, me]
        for peer in ready[:-1]:
            send_tile(h, peer)

    for h in range(PARTS):
        wait_all(in_a[h], h, a_recv)
        if h == PARTS - 1:
            middle_stage()
        code_part(h)
    for h in range(PARTS):
        wait_all(out_a.at[h], h, a_send)

    def arrived(h):
        wait_all(out_b.at[h], h, b_send)
        wait_all(tiles[h], h, b_recv)
        wait_all(unit_out.at[h], h, c_send)
        wait_all(unit_in[h], h, c_recv)

    def right_hand_side(h):
        rows_of = pl.ds(h * part, part)

        def add_tiles(i, running):
            places = [i * GROUP + j for j in range(GROUP)]
            spots = [jnp.clip(table[0, j], 0, slots - 1) for j in places]
            terms = [
                tiles[h][spot].astype(jnp.int32).astype(F32) * unit_in[h][spot] for spot in spots
            ]
            for j, term in zip(places, terms):
                running = running * table[1, j].astype(F32) + term
                red[j, rows_of] = running
            return running

        lax.fori_loop(0, slots // GROUP, add_tiles, jnp.zeros((part, rows), F32))

        @pl.loop(0, count // 2)
        def _(i):
            for g in (2 * i, 2 * i + 1):
                last = jnp.clip(table[2, g], 0, slots - 1)
                res[0, g, rows_of] = red[last, rows_of] * table[3, g].astype(F32)

    for h in range(PARTS):
        arrived(h)
        right_hand_side(h)

    theta = finish()
    theta = jnp.sum(jnp.sum(theta, axis=0, keepdims=True), axis=1, keepdims=True)
    inv[...] = jnp.broadcast_to((1.0 * devices * count * rows) / theta, inv.shape)

    def precondition(blocks, k, fields):
        outs = [
            product(stacked(field), wp[g], values) + field * diag_p[g]
            for g, field in zip(blocks, fields)
        ]
        for g, out in zip(blocks, outs):
            red[k * count + g] = out
            xs[k % 2, g + 1] = stacked(out)

    def apply_blocks(blocks, k, operands):
        fields = [red[k * count + g] for g in blocks]
        nows = [res[k, g] for g in blocks]
        befores = [res[k - 1, g] for g in blocks] if k > 0 else None
        images = [
            product(operand, wa[g], values) + field * diag_a[g]
            for g, field, operand in zip(blocks, fields, operands)
        ]
        laters = [now - image * inv[0:1] for now, image in zip(nows, images)]
        steps = [now - later for now, later in zip(nows, laters)]

        def dots(slot, left, right):
            acc[slot] += sum(a * b for a, b in zip(left, right))

        if k + 1 < STEPS:
            precondition(blocks, k + 1, laters)
        for g, later in zip(blocks, laters):
            res[k + 1, g] = later
        if k == 0:
            dots(0, fields, steps)
        else:
            dots(2 * k - 1, fields, [x - y for x, y in zip(befores, nows)])
            dots(2 * k, fields, steps)
        if k == 2:
            dots(5, [red[g] for g in blocks], laters)
            dots(6, [red[count + g] for g in blocks], laters)
            dots(7, fields, laters)

    def inner(g, k, width):
        near = [xs[k % 2, g + i] for i in range(width + 2)]
        apply_blocks(
            tuple(g + i for i in range(width)),
            k,
            [
                jnp.concatenate([near[i + 1], near[i + 2], near[i]], axis=1)
                for i in range(width)
            ],
        )

    def inners(start, stop, k):
        whole = (stop - start) // BATCH

        @pl.loop(0, whole)
        def _(i):
            inner(start + BATCH * i, k, BATCH)

        if (stop - start) % BATCH:
            inner(start + BATCH * whole, k, (stop - start) % BATCH)

    def preconditions(start, stop):
        whole = (stop - start) // BATCH

        def some(g, width):
            blocks = tuple(g + i for i in range(width))
            precondition(blocks, 0, [res[0, block] for block in blocks])

        @pl.loop(0, whole)
        def _(i):
            some(start + BATCH * i, BATCH)

        if (stop - start) % BATCH:
            some(start + BATCH * whole, (stop - start) % BATCH)

    def halo_copy(k, side):
        return pltpu.make_async_remote_copy(
            src_ref=xs.at[k % 2, count if side == 0 else 1],
            dst_ref=halo.at[k, side],
            send_sem=halo_send.at[k, side],
            recv_sem=halo_recv.at[k, side],
            device_id=after_id if side == 0 else before_id,
            device_id_type=MESH,
        )

    edges = (0, count - 1)
    middle = count // 2 + 1
    acc[...] = jnp.zeros_like(acc)
    precondition(edges, 0, [res[0, g] for g in edges])
    preconditions(1, 9)
    halo_copy(0, 0).start()
    halo_copy(0, 1).start()
    preconditions(9, count - 1)

    link_copy.wait()
    for k in range(STEPS):
        inners(1, middle, k)
        halo_copy(k, 0).wait()
        halo_copy(k, 1).wait()
        buf = k % 2
        apply_blocks(
            edges,
            k,
            [
                jnp.concatenate([xs[buf, 1], xs[buf, 2], halo[k, 0]], axis=1),
                jnp.concatenate([xs[buf, count], halo[k, 1], xs[buf, count - 1]], axis=1),
            ],
        )
        inners(middle, middle + 4, k)
        if k + 1 < STEPS:
            halo_copy(k + 1, 0).start()
            halo_copy(k + 1, 1).start()
        inners(middle + 4, count - 1, k)

    lane = lax.broadcasted_iota(jnp.int32, (values, rows), 1)
    packed = jnp.zeros((values, rows), F32)
    for j in range(8):
        packed = packed + jnp.where(lane == j, jnp.sum(acc[j], axis=1, keepdims=True), 0.0)
    packed = jnp.concatenate([packed, jnp.zeros((rows - values, rows), F32)], axis=0)
    begin, middle_stage, finish = reduce_over(1, packed.T[0:8])
    begin()
    middle_stage()
    total = finish()

    def over(top, bottom):
        usable = bottom != 0.0
        return jnp.where(usable, top / jnp.where(usable, bottom, 1.0), 0.0)

    g00, g10, g11, g21, g22 = (total[j : j + 1] for j in range(5))
    h0, h1, h2 = (-total[j : j + 1] for j in range(5, 8))
    l1, l2 = over(g10, g00), over(g11, g00)
    d1 = g11 - l1 * g10
    mix = g21 - l2 * g10
    l3 = over(mix, d1)
    d2 = g22 - l2 * g11 - l3 * mix
    y1 = h1 - l1 * h0
    y2 = h2 - l2 * h0 - l3 * y1
    e2 = over(y2, d2)
    e1 = over(y1, d1) - l3 * e2
    e0 = over(h0, g00) - l1 * e1 - l2 * e2
    weights = jnp.concatenate([e0, e1, e2, jnp.zeros((rows - 3, rows), F32)], axis=0).T
    e0 = jnp.broadcast_to(weights[0:values, 0:1], (values, rows))
    e1 = jnp.broadcast_to(weights[0:values, 1:2], (values, rows))
    e2 = jnp.broadcast_to(weights[0:values, 2:3], (values, rows))
    scale = inv[0:1]
    for j, factor in enumerate(
        ((1.0 - e0) * scale, (1.0 - e1) * scale, (1.0 - e2) * scale, e0, e1 - e0, e2 - e1, 1.0 - e2)
    ):
        mix_ref[j] = factor


def combine_kernel(res, red, mix_ref, x_hbm, res_hbm, x_all, r_all, sems):
    count, values, rows = x_all.shape
    pieces = count // PIECE

    def puts(piece):
        part = pl.ds(piece * PIECE, PIECE)
        return (
            pltpu.make_async_copy(x_all.at[part], x_hbm.at[part], sems.at[0, piece]),
            pltpu.make_async_copy(r_all.at[part], res_hbm.at[part], sems.at[1, piece]),
        )

    @pl.loop(0, pieces)
    def _(piece):
        for top in range(0, values, SUBLANES):
            some = pl.ds(top, SUBLANES)
            x0, x1, x2, r0, r1, r2, r3 = (mix_ref[j, some] for j in range(7))
            for i in range(PIECE):
                g = piece * PIECE + i
                x_all[g, some] = (
                    x0 * red[g, some] + x1 * red[count + g, some] + x2 * red[2 * count + g, some]
                )
                r_all[g, some] = (
                    r0 * res[0, g, some]
                    + r1 * res[1, g, some]
                    + r2 * res[2, g, some]
                    + r3 * res[3, g, some]
                )

        for put in puts(piece):
            put.start()

    @pl.loop(0, pieces)
    def _(piece):
        for put in puts(piece):
            put.wait()


def mass_solve(target, links, pick, live, relay, history, mixed, mass_diag, mass_next, precond):
    doms, subs = lax.axis_size("dom"), lax.axis_size("sub")
    slots = mixed.shape[0]
    blocks, values, rows = history.shape
    count = mass_diag.shape[0]
    shape = (doms, subs, count, values, rows, slots)

    def kernel(*refs):
        solve_kernel(shape, *refs)

    smem = pl.BlockSpec(memory_space=pltpu.SMEM)
    hbm = pl.BlockSpec(memory_space=pl.ANY)
    field = jax.ShapeDtypeStruct((count, values, rows), F32)
    dma = pltpu.SemaphoreType.DMA
    vmem = pl.BlockSpec(memory_space=pltpu.VMEM)
    parts = (
        pltpu.VMEM((STEPS + 1, count, values, rows), F32),
        pltpu.VMEM((STEPS * count, values, rows), F32),
        pltpu.VMEM((7, values, rows), F32),
    )
    parts = pl.pallas_call(
        kernel,
        out_shape=parts,
        in_specs=[pl.BlockSpec(memory_space=pltpu.VMEM)] + [smem] * 4 + [hbm] * 5,
        out_specs=(vmem,) * 3,
        scratch_shapes=[
            pltpu.VMEM((blocks, values, rows), BF16),
            pltpu.VMEM((slots, rows, rows), BF16),
            pltpu.VMEM((PARTS, slots, values // PARTS, rows), BF16),
            pltpu.VMEM((slots, values // PARTS, rows), BF16),
            pltpu.VMEM((slots, values // PARTS, rows), BF16),
            pltpu.VMEM((PARTS, slots, values // PARTS, rows), jnp.int16),
            pltpu.VMEM((slots, values // PARTS, rows), jnp.int16),
            pltpu.VMEM((slots, values // PARTS, rows), jnp.int16),
            pltpu.VMEM((PARTS, slots, 1, rows), F32),
            pltpu.VMEM((slots, 1, rows), F32),
            pltpu.VMEM((slots, 1, rows), F32),
            pltpu.VMEM((2, 3, CHUNK, rows, rows), F32),
            pltpu.VMEM((count + 1, 3 * rows, 2 * rows), BF16),
            pltpu.VMEM((count, rows, 2 * rows), BF16),
            pltpu.VMEM((count, 1, rows), F32),
            pltpu.VMEM((count, 1, rows), F32),
            pltpu.VMEM((2, count + 2, 2 * values, rows), BF16),
            pltpu.VMEM((STEPS, 2, 2 * values, rows), BF16),
            pltpu.VMEM((8, values, rows), F32),
            pltpu.VMEM((8, rows), F32),
            pltpu.VMEM((8, rows), F32),
            pltpu.VMEM((2, 2, 8, rows), F32),
            pltpu.VMEM((2, doms, 8, rows), F32),
            pltpu.VMEM((2, subs, 8, rows), F32),
            pltpu.VMEM((8, rows), jnp.int32),
            pltpu.SMEM((8, rows), jnp.int32),
            dma,
            pltpu.SemaphoreType.REGULAR((2,)),
            dma,
            dma,
            dma((PARTS,)),
            dma((PARTS,)),
            dma((PARTS,)),
            dma((PARTS,)),
            dma((PARTS,)),
            dma((PARTS,)),
            dma((2, 3)),
            dma((STEPS, 2)),
            dma((STEPS, 2)),
            dma,
            dma,
            dma((2, doms)),
            dma((2, doms)),
            dma((2, subs)),
            dma((2, subs)),
        ],
        compiler_params=pltpu.CompilerParams(
            collective_id=0, has_side_effects=True, vmem_limit_bytes=LIMIT1 * 1024
        ),
    )(target, links, pick, live, relay, history, mixed, mass_diag, mass_next, precond)
    return pl.pallas_call(
        combine_kernel,
        out_shape=(field, field),
        in_specs=[vmem] * 3,
        out_specs=(hbm, hbm),
        scratch_shapes=[
            pltpu.VMEM((count, values, rows), F32),
            pltpu.VMEM((count, values, rows), F32),
            dma((2, count // PIECE)),
        ],
        compiler_params=pltpu.CompilerParams(vmem_limit_bytes=LIMIT2 * 1024),
    )(*parts)


def body(
    history,
    send_list,
    send_count,
    mixed_mass,
    relay_list,
    relay_target,
    mass_diag,
    mass_next,
    coupling,
    precond,
):
    return mass_solve(
        relay_target.reshape(1, -1),
        coupling,
        send_list.reshape(-1),
        send_count.reshape(-1),
        relay_list.reshape(-1),
        history,
        mixed_mass,
        mass_diag,
        mass_next,
        precond,
    )


def solution(mesh):
    whole = ("dom", "sub")
    placed = (
        P(whole, None, None),
        P(whole, None, None),
        P(whole, None),
        P(whole, None, None),
        P(whole, None, None),
        P(whole, None, None),
        P(whole, None, None),
        P(whole, None, None),
        P(whole),
        P(whole, None, None),
    )
    return jax.shard_map(
        body,
        mesh=mesh,
        in_specs=placed,
        out_specs=(P(whole, None, None), P(whole, None, None)),
        check_vma=False,
    )
```
